32 devices in a mesh: freq: 2 (over y), tile: 8 (over z, x), src: 2 (over core).
Axes of the slice: x: 2, y: 2, z: 4, core: 2. Of those that a mesh axis runs over, the one named last changes fastest.
Arguments:
- green: bfloat16 [2, 4096, 1024], P(None, ('freq', 'tile'), 'src'), parts along dimension 1, may hold values from -0.1875 to 0.1875
- direction: bfloat16 [2, 2048, 1024], P(None, ('freq', 'src')), parts along dimension 1, may hold values from -6 to 6
- partners: int32 [32, 8], P(('freq', 'tile')), parts along dimension 0, may hold values from 0 to 15, as said below
- counts: int32 [32], P(('freq', 'tile')), parts along dimension 0, may hold values from 1 to 8, as said below
Outputs:
- hessian: float32 [2048, 2, 1024], P(('freq', 'tile'), None, 'src'), parts along dimension 0
The draws below stay inside these ranges and needn't reach their ends.
There are 2 independent parts, one for each index of `freq`. The reference program is written for one: setup_inputs(seed, part) draws one part's arguments, and reference() takes and returns one part's arrays. A program takes and returns all parts, laid end to end along the dimension named above; each array names one. Nothing has to cross between parts.
Inputs may be any that keep to these rules, and one draw needn't show every extreme that they name: The entries partners[t, k] of a row are distinct tile indices u with |u // 2 - t // 2| <= 3; only those with k < counts[t] are sampled. `counts`: some tile row has all 8 slots sampled, and some tile row has only one.
All inputs are finite; a program needn't handle non-finite values.
Results may differ from the reference program's by a relative error of at most 0.0016.
Values may be sent and summed in bfloat16 or wider, within the bound.
A program may use at most 64 MiB of HBM per device.

```python
import jax
import jax.numpy as jnp
from jax import lax

TILE = 128
SRC = 1024
TILE_DEV = 2
BAND_DEV = 3
TILES = 16
SENSORS = 2048
KMAX = 8


def pattern_tables(key):
    base_key = jax.random.fold_in(key, 4711)
    key_score, key_left, key_right, key_top, key_bottom = jax.random.split(base_key, 5)
    width = (2 * BAND_DEV + 1) * TILE_DEV
    rows = jnp.arange(TILES, dtype=jnp.int32)
    first = (rows // TILE_DEV - BAND_DEV) * TILE_DEV
    candidate = first[:, None] + jnp.arange(width, dtype=jnp.int32)[None, :]
    inside = (candidate >= 0) & (candidate < TILES)
    score = jax.random.randint(key_score, (TILES, width), 0, 2 ** 20, dtype=jnp.int32) * width
    score = score + jnp.arange(width, dtype=jnp.int32)[None, :]
    score = jnp.where(inside, score, score + 2 ** 26)
    order = jnp.argsort(score, axis=1, stable=True)[:, :KMAX]
    partner_table = jnp.take_along_axis(candidate, order, axis=1).astype(jnp.int32)
    left = jax.random.randint(key_left, (TILES,), 0, KMAX, dtype=jnp.int32)
    right = jax.random.randint(key_right, (TILES,), 0, KMAX, dtype=jnp.int32)
    count_table = jnp.maximum(1, KMAX - left * right // (KMAX - 1))
    top = jax.random.randint(key_top, (), 0, TILES, dtype=jnp.int32)
    bottom = (top + 1 + jax.random.randint(key_bottom, (), 0, TILES - 1, dtype=jnp.int32)) % TILES
    count_table = jnp.where(rows == top, KMAX, count_table)
    count_table = jnp.where(rows == bottom, 1, count_table).astype(jnp.int32)
    return (partner_table, count_table)


def draw_partners(key, part):
    return pattern_tables(key)[0]


def draw_counts(key, part):
    return pattern_tables(key)[1]


def levels(rng, extent, cuts, smallest, largest):
    def one(dim, shards_of):
        draws = jax.random.uniform(jax.random.fold_in(jax.random.fold_in(rng, 6), dim), (shards_of,), jnp.float32, smallest / len(cuts), largest / len(cuts))
        return jnp.repeat(jnp.exp(draws), extent[dim] // shards_of).reshape((-1,) + (1,) * (len(extent) - dim - 1))

    loudness = one(*cuts[0])
    for cut in cuts[1:]:
        loudness = loudness * one(*cut)
    return loudness


def noise(key, dims, scale, reach, cuts=(), kind=jnp.bfloat16):
    loudness = levels(key, dims, cuts, -0.22, 0.18) if cuts else 1.0
    array = jax.random.normal(key, dims, jnp.float32) * scale * loudness
    return jnp.minimum(jnp.maximum(array, -reach), reach).astype(kind)


def setup_inputs(seed: int = 0, part: int = 0) -> dict:
    key_of = jax.random.split(jax.random.key(seed), 5)
    part_splits = jax.random.split(jax.random.fold_in(key_of[4], part), 5)
    green = noise(part_splits[0], (2, SENSORS, SRC), SRC ** -0.5, 0.1875, ((1, 8), (2, 2)))
    direction = noise(part_splits[1], (2, SRC, SRC), 1.0, 6.0, ((1, 2),))
    partners = draw_partners(jax.random.fold_in(jax.random.fold_in(key_of[4], part), 71), part)
    counts = draw_counts(jax.random.fold_in(jax.random.fold_in(key_of[4], part), 71), part)
    return {"green": green, "direction": direction, "partners": partners, "counts": counts}


def reference(green, direction, partners, counts):
    sources = green.shape[2]
    tiles = green.reshape(2, TILES, TILE, sources)
    live = (jnp.arange(KMAX, dtype=jnp.int32)[None, :] < counts[:, None]).astype(jnp.float32)

    def visit(total, index):
        own = lax.dynamic_index_in_dim(tiles, index, 1, keepdims=False)
        image_real = (jnp.dot(own[0], direction[0], preferred_element_type=jnp.float32)
                      - jnp.dot(own[1], direction[1], preferred_element_type=jnp.float32)).astype(jnp.bfloat16)
        image_imag = (jnp.dot(own[0], direction[1], preferred_element_type=jnp.float32)
                      + jnp.dot(own[1], direction[0], preferred_element_type=jnp.float32)).astype(jnp.bfloat16)
        stack = jnp.take(tiles, partners[index].astype(jnp.int32), axis=1).reshape(2, KMAX * TILE, sources)
        mask = jnp.repeat(live[index], TILE)[None, :]
        couple_real = (jnp.dot(image_real, stack[0].T, preferred_element_type=jnp.float32)
                       + jnp.dot(image_imag, stack[1].T, preferred_element_type=jnp.float32))
        couple_imag = (jnp.dot(image_imag, stack[0].T, preferred_element_type=jnp.float32)
                       - jnp.dot(image_real, stack[1].T, preferred_element_type=jnp.float32))
        couple_real = (couple_real * mask).astype(jnp.bfloat16)
        couple_imag = (couple_imag * mask).astype(jnp.bfloat16)
        weight_real = (jnp.dot(couple_real, stack[0], preferred_element_type=jnp.float32)
                       - jnp.dot(couple_imag, stack[1], preferred_element_type=jnp.float32)).astype(jnp.bfloat16)
        weight_imag = (jnp.dot(couple_real, stack[1], preferred_element_type=jnp.float32)
                       + jnp.dot(couple_imag, stack[0], preferred_element_type=jnp.float32)).astype(jnp.bfloat16)
        out_real = (jnp.dot(own[0].T, weight_real, preferred_element_type=jnp.float32)
                    + jnp.dot(own[1].T, weight_imag, preferred_element_type=jnp.float32))
        out_imag = (jnp.dot(own[0].T, weight_imag, preferred_element_type=jnp.float32)
                    - jnp.dot(own[1].T, weight_real, preferred_element_type=jnp.float32))
        return total + jnp.stack([out_real, out_imag], axis=1), None

    start = jnp.zeros((sources, 2, sources), jnp.float32)
    total, _ = lax.scan(visit, start, jnp.arange(TILES, dtype=jnp.int32))
    return total
```

```python
import functools

import jax
import jax.numpy as jnp
from jax import lax
from jax.experimental import pallas as pl
from jax.experimental.pallas import tpu as pltpu
from jax.sharding import PartitionSpec as P

BAND_DEV = 3
PIECES = 8
CHUNKS = 4
OWN, ACROSS, NEAR, BACK, BACK_ACROSS, NEAR_ACROSS, FAR, PAIR, PAIR_ACROSS = range(9)
OFFSETS = (0, 1, 2, -2, -1, 3, -3)
ROUTES = (
    (OWN, ACROSS),
    (OWN, BACK),
    (OWN, NEAR),
    (ACROSS, NEAR_ACROSS),
    (NEAR, BACK_ACROSS),
    (BACK_ACROSS, FAR),
)
F32 = jnp.float32
BF16 = jnp.bfloat16


def dot(left, right, dims):
    return lax.dot_general(left, right, (dims, ((), ())), preferred_element_type=F32)


def short_line(out_rows, levels):
    return out_rows % 128 == 0 and levels <= 4


def kernel(
    count_tile, a_ref, v_ref, partners_ref, counts_ref, out_ref,
    table, sampled, win, vbuf, img, ipart, irecv, cpart, crecv, acc, w, turned, rr, hp, hr,
    load_sem, img_sem, route_send, route_recv, couple_send, couple_recv,
    pair_send, pair_recv, w_send, w_recv, h_send, h_recv, o_send, tot,
):
    me = lax.axis_index("tile")
    core = lax.axis_index("src")
    side = lax.rem(me, 2)
    level = me // 2
    levels = count_tile // 2
    step = 1 - 2 * side
    rows, half = win.shape[2], win.shape[3]
    tiles, kmax = table.shape
    out_rows = out_ref.shape[0]
    wide = half // CHUNKS

    def inside(place):
        return (place >= 0) & (place < levels)

    has_near = inside(level + step)
    has_back = inside(level - step)
    has_far = inside(level - 2 * step)
    across = {"tile": me + step}
    forward = {"tile": me + 2 * step}
    backward = {"tile": me - 2 * step}
    partner = {"src": 1 - core}
    targets = (across, forward, backward, backward, across, forward)
    sends = (None, has_near, has_back, has_back, has_near, has_near & has_back)
    arrives = (None, has_back, has_near, has_near, has_back, has_far)

    def guarded(condition, run):
        if condition is None:
            run()
        else:
            pl.when(condition)(run)

    def remote(source, target, send, recv, device):
        return pltpu.make_async_remote_copy(
            src_ref=source, dst_ref=target, send_sem=send, recv_sem=recv,
            device_id=device, device_id_type=pl.DeviceIdType.MESH,
        )

    def piece(slot, index):
        depth = 2 * rows // PIECES
        per = PIECES // 2
        return win.at[slot, index // per, pl.ds((index % per) * depth, depth)]

    def route(number, index):
        source, target = ROUTES[number]
        return remote(
            piece(source, index), piece(target, index),
            route_send.at[number, index], route_recv.at[number, index], targets[number],
        )

    def send_route(number, index):
        guarded(sends[number], lambda: route(number, index).start())

    def arrive(number, index):
        guarded(arrives[number], lambda: route(number, index).wait_recv())

    def to_pair(source, target, number):
        return remote(win.at[source], win.at[target], pair_send.at[number], pair_recv.at[number], partner)

    load_a = pltpu.make_async_copy(a_ref, win.at[OWN], load_sem.at[0])
    load_theirs = pltpu.make_async_copy(
        v_ref.at[:, :, pl.ds(pl.multiple_of((1 - core) * half, half), half)], vbuf.at[0], load_sem.at[1]
    )
    load_mine = pltpu.make_async_copy(
        v_ref.at[:, :, pl.ds(pl.multiple_of(core * half, half), half)], vbuf.at[1], load_sem.at[2]
    )
    load_table = pltpu.make_async_copy(partners_ref, table, load_sem.at[3])
    load_counts = pltpu.make_async_copy(counts_ref, sampled, load_sem.at[4])
    load_a.start()
    load_table.start()
    load_counts.start()
    load_theirs.start()
    load_mine.start()

    barrier = pltpu.get_barrier_semaphore()
    pl.semaphore_signal(barrier, inc=1, device_id=partner, device_id_type=pl.DeviceIdType.MESH)
    pl.semaphore_signal(barrier, inc=1, device_id=across, device_id_type=pl.DeviceIdType.MESH)

    def other_level(number):
        return lax.rem(level + 1 + number, levels)

    if short_line(out_rows, levels):
        for there, device in ((has_near, forward), (has_back, backward)):
            @pl.when(there)
            def _(device=device):
                pl.semaphore_signal(barrier, inc=1, device_id=device, device_id_type=pl.DeviceIdType.MESH)

        pl.semaphore_wait(barrier, 2 + has_near.astype(jnp.int32) + has_back.astype(jnp.int32))
    else:
        @pl.loop(0, levels - 1)
        def _(number):
            pl.semaphore_signal(
                barrier, inc=1, device_id={"tile": other_level(number) * 2 + side},
                device_id_type=pl.DeviceIdType.MESH,
            )

        pl.semaphore_wait(barrier, levels + 1)
    load_a.wait()
    for index in range(PIECES):
        for number in (0, 1, 2):
            send_route(number, index)
    to_pair(OWN, PAIR, 0).start()

    own = win[OWN].reshape(2 * rows, half)

    def images(slot):
        first = dot(own, vbuf[slot, 0], ((1,), (0,)))
        second = dot(own, vbuf[slot, 1], ((1,), (0,)))
        return first[:rows] - second[rows:], second[:rows] + first[rows:]

    load_theirs.wait()
    real, imag = images(0)
    ipart[0] = real
    ipart[1] = imag
    image_copy = remote(ipart, irecv, img_sem.at[0], img_sem.at[1], partner)
    image_copy.start()
    load_mine.wait()
    real, imag = images(1)
    image_copy.wait_recv()
    img[:rows] = (real + irecv[0]).astype(BF16)
    img[rows:] = (imag + irecv[1]).astype(BF16)

    load_table.wait()
    load_counts.wait()
    acc[...] = jnp.zeros_like(acc)

    def exists(slot):
        return (
            (slot <= ACROSS)
            | (((slot == NEAR) | (slot == NEAR_ACROSS)) & has_near)
            | (((slot == BACK) | (slot == BACK_ACROSS)) & has_back)
            | ((slot == FAR) & has_far)
        )

    def sample(slot):
        offset = 0
        for index, value in enumerate(OFFSETS):
            offset = jnp.where(slot == index, value, offset)
        first = (me + offset * step) * tiles
        tile = rows // tiles
        bands = []
        for row in range(tiles):
            blocks = []
            for column in range(tiles):
                hit = False
                for k in range(kmax):
                    hit = hit | ((table[row, k] == first + column) & (k < sampled[row]))
                blocks.append(jnp.full((tile, tile), jnp.where(hit, 1.0, 0.0), F32))
            bands.append(jnp.concatenate(blocks, axis=1))
        return jnp.concatenate(bands, axis=0)

    def couple_copy(slot):
        return remote(cpart.at[slot], crecv.at[slot], couple_send.at[slot], couple_recv.at[slot], partner)

    def couple(low, high):
        @pl.loop(low, high)
        def _(slot):
            @pl.when(exists(slot))
            def _():
                block = win[slot].reshape(2 * rows, half)
                prod = dot(img[...], block, ((1,), (1,)))
                cpart[slot, 0] = prod[:rows, :rows] + prod[rows:, rows:]
                cpart[slot, 1] = prod[rows:, :rows] - prod[:rows, rows:]
                couple_copy(slot).start()

    def weigh(low, high):
        @pl.loop(low, high)
        def _(slot):
            @pl.when(exists(slot))
            def _():
                couple_copy(slot).wait_recv()
                live = sample(slot)
                real = ((cpart[slot, 0] + crecv[slot, 0]) * live).astype(BF16)
                imag = ((cpart[slot, 1] + crecv[slot, 1]) * live).astype(BF16)
                left = jnp.concatenate(
                    [jnp.concatenate([real, -imag], axis=1), jnp.concatenate([imag, real], axis=1)], axis=0
                )
                acc[...] += dot(left, win[slot].reshape(2 * rows, half), ((1,), (0,)))

    def pass_on(index):
        arrive(0, index)
        send_route(3, index)
        arrive(2, index)
        send_route(4, index)

    couple(OWN, ACROSS)
    for index in range(PIECES):
        pass_on(index)
    to_pair(ACROSS, PAIR_ACROSS, 1).start()
    for index in range(PIECES):
        arrive(1, index)
    span = max(out_rows, 128)

    def turn_over():
        to_pair(OWN, PAIR, 0).wait_recv()
        to_pair(ACROSS, PAIR_ACROSS, 1).wait_recv()

        @pl.loop(0, turned.shape[0])
        def _(group):
            column = (2 * group + side) * out_rows if span == out_rows else group * span
            which = column // half
            base = jnp.where(which == core, OWN, PAIR)
            lanes = pl.ds(pl.multiple_of(column - which * half, 128), span)
            for block in range(2):
                turned[group, :, block * 2 * rows : (block + 1) * 2 * rows] = (
                    win[base + block, :, :, lanes].reshape(2 * rows, span).T
                )

    jobs = (
        lambda: couple(ACROSS, BACK_ACROSS),
        lambda: weigh(OWN, NEAR),
        lambda: weigh(NEAR, BACK_ACROSS),
        turn_over,
    )
    for index in range(PIECES):
        for job in jobs[index * len(jobs) // PIECES : (index + 1) * len(jobs) // PIECES]:
            job()
        arrive(4, index)
        send_route(5, index)
    couple(BACK_ACROSS, NEAR_ACROSS)
    for index in range(PIECES):
        arrive(3, index)
    couple(NEAR_ACROSS, FAR)
    weigh(BACK_ACROSS, NEAR_ACROSS)
    for index in range(PIECES):
        arrive(5, index)
    couple(FAR, FAR + 1)
    weigh(NEAR_ACROSS, FAR + 1)

    def w_copy(chunk):
        return remote(w.at[chunk, 0], w.at[chunk, 1], w_send.at[chunk], w_recv.at[chunk], across)

    for chunk in range(CHUNKS):
        w[chunk, 0] = acc[:, chunk * wide : (chunk + 1) * wide].astype(BF16)
        w_copy(chunk).start()
    def partial(chunk, group):
        return dot(turned[group], rr[chunk], ((1,), (0,)))

    def rows_of(target):
        return pl.multiple_of((2 * target + side) * out_rows, out_rows)

    def prepare(chunk):
        for block in range(2):
            if block:
                w_copy(chunk).wait_recv()
            top, low = w[chunk, block, :rows], w[chunk, block, rows:]
            first = 2 * rows * block
            rr[chunk, first : first + rows] = jnp.concatenate([top, low], axis=1)
            rr[chunk, first + rows : first + 2 * rows] = jnp.concatenate([low, -top], axis=1)

    def put(chunk, total):
        for part in range(2):
            for index in range(wide // 128):
                first = part * wide + index * 128
                out_ref[:, 2 * (chunk * wide // 128 + index) + part] = total[:, first : first + 128]

    def term(chunk, lane, slot, target, level_to):
        return remote(
            hp.at[chunk, pl.ds(rows_of(target), out_rows)], hr.at[chunk, lane, slot],
            h_send.at[chunk, target], h_recv.at[chunk, lane, slot], {"tile": 2 * level_to + side},
        )

    def onward(chunk, lane, target):
        return remote(
            hr.at[chunk, lane, target], hr.at[chunk, lane, target],
            o_send.at[chunk], h_recv.at[chunk, lane, target], {"tile": 2 * target + side},
        )

    if short_line(out_rows, levels):
        depths = level, levels - 1 - level

        def total(chunk):
            prepare(chunk)
            every = turned[...].reshape(levels * out_rows, 4 * rows)
            tot[chunk] = dot(every, rr[chunk], ((1,), (0,))).reshape(levels, out_rows, 2 * wide)

        def place(target):
            return pl.ds(rows_of(target), out_rows)

        def far(lane, number):
            return levels - 1 - number if lane == 0 else number

        def passing(chunk, lane, target):
            return term(chunk, lane, target, target, level + 1 - 2 * lane)

        def begin(chunk, numbers):
            for lane in range(2):
                for number in numbers:
                    target = far(lane, number)

                    @pl.when(depths[lane] == 0)
                    def _(lane=lane, target=target):
                        hp[chunk, place(target)] = tot[chunk, target].astype(BF16)
                        passing(chunk, lane, target).start()

        def beside(chunk):
            for lane in range(2):
                target = far(lane, 0)

                @pl.when(depths[lane] == 2)
                def _(lane=lane, target=target):
                    hp[chunk, place(target)] = tot[chunk, target].astype(BF16)
                    term(chunk, lane, levels, target, target).start()

        def add_on(chunk, number):
            for lane in range(2):
                target = far(lane, number)

                @pl.when(depths[lane] == 1)
                def _(lane=lane, target=target):
                    passing(chunk, lane, target).wait_recv()
                    hp[chunk, place(target)] = (
                        tot[chunk, target] + hr[chunk, lane, target].astype(F32)
                    ).astype(BF16)
                    passing(chunk, lane, target).start()

        def relay(chunk):
            for lane in range(2):
                target = far(lane, 0)

                @pl.when(depths[lane] == 2)
                def _(lane=lane, target=target):
                    passing(chunk, lane, target).wait_recv()
                    onward(chunk, lane, target).start()

        distant = range(levels - 2)

        for chunk in range(CHUNKS + 3):
            if chunk < CHUNKS:
                total(chunk)
                begin(chunk, distant)
                if levels > 3:
                    beside(chunk)
            if chunk == CHUNKS - 1 and levels > 1:
                for done in range(CHUNKS):
                    begin(done, (levels - 2,))
            for number in distant:
                if 0 <= chunk - 1 < CHUNKS:
                    add_on(chunk - 1, number)
                if number == 0 and levels > 3 and 0 <= chunk - 2 < CHUNKS:
                    relay(chunk - 2)

        for chunk in range(CHUNKS):
            for lane, slot, there in (
                (0, level, depths[0] > 0), (1, level, depths[1] > 0),
                (0, levels, depths[0] > 2), (1, levels, depths[1] > 2),
            ):
                @pl.when(there)
                def _(chunk=chunk, lane=lane, slot=slot):
                    term(chunk, lane, slot, level, level).wait_recv()
                    tot[chunk, level] += hr[chunk, lane, slot].astype(F32)
            put(chunk, tot[chunk, level])
    else:
        for chunk in range(CHUNKS):
            prepare(chunk)
            if span != out_rows:
                @pl.loop(0, hp.shape[1] // span)
                def _(group):
                    column = pl.multiple_of(group * span, span)
                    hp[chunk, pl.ds(column, span)] = partial(chunk, group).astype(BF16)

            @pl.loop(0, levels - 1)
            def _(number):
                target = other_level(number)
                if span == out_rows:
                    hp[chunk, pl.ds(rows_of(target), out_rows)] = partial(chunk, target).astype(BF16)
                term(chunk, 0, level, target, target).start()

            if span == out_rows:
                hp[chunk, pl.ds(rows_of(level), out_rows)] = partial(chunk, level).astype(BF16)

        for chunk in range(CHUNKS):
            def add(number, total):
                sender = other_level(number)
                term(chunk, 0, sender, level, sender).wait_recv()
                return total + hr[chunk, 0, sender].astype(F32)

            put(chunk, lax.fori_loop(0, levels - 1, add, hp[chunk, pl.ds(rows_of(level), out_rows)].astype(F32)))

    for number in range(len(ROUTES)):
        for index in range(PIECES):
            guarded(sends[number], lambda number=number, index=index: route(number, index).wait_send())
    to_pair(OWN, PAIR, 0).wait_send()
    to_pair(ACROSS, PAIR_ACROSS, 1).wait_send()
    image_copy.wait_send()

    @pl.loop(0, FAR + 1)
    def _(slot):
        @pl.when(exists(slot))
        def _():
            couple_copy(slot).wait_send()

    for chunk in range(CHUNKS):
        w_copy(chunk).wait_send()

        @pl.loop(0, levels - 1)
        def _(number):
            target = other_level(number)
            term(chunk, 0, target, target, target).wait_send()

        if short_line(out_rows, levels) and levels > 3:
            @pl.when((level == 2) | (levels - 1 - level == 2))
            def _(chunk=chunk):
                onward(chunk, 0, 0).wait_send()


def shards(count_tile, green, direction, partners, counts):
    tile_dev, kmax = partners.shape
    rows, half = green.shape[1:]
    sources = direction.shape[2]
    out_rows = sources // count_tile
    levels = count_tile // 2
    wide = half // CHUNKS
    lanes = 2 if short_line(out_rows, levels) else 1
    anywhere = pl.BlockSpec(memory_space=pl.ANY)
    local = pl.BlockSpec(memory_space=pltpu.VMEM)
    dma = pltpu.SemaphoreType.DMA
    out = pl.pallas_call(
        functools.partial(kernel, count_tile),
        out_shape=jax.ShapeDtypeStruct((out_rows, half // 64, 128), F32),
        in_specs=[anywhere] * 4,
        out_specs=local,
        scratch_shapes=[
            pltpu.SMEM((tile_dev, kmax), jnp.int32),
            pltpu.SMEM((tile_dev,), jnp.int32),
            pltpu.VMEM((9, 2, rows, half), BF16),
            pltpu.VMEM((2, 2, half, half), BF16),
            pltpu.VMEM((2 * rows, half), BF16),
            pltpu.VMEM((2, rows, half), F32),
            pltpu.VMEM((2, rows, half), F32),
            pltpu.VMEM((FAR + 1, 2, rows, rows), F32),
            pltpu.VMEM((FAR + 1, 2, rows, rows), F32),
            pltpu.VMEM((2 * rows, half), F32),
            pltpu.VMEM((CHUNKS, 2, 2 * rows, wide), BF16),
            pltpu.VMEM((levels if out_rows >= 128 else sources // 128, max(out_rows, 128), 4 * rows), BF16),
            pltpu.VMEM((CHUNKS, 4 * rows, 2 * wide), BF16),
            pltpu.VMEM((CHUNKS, sources, 2 * wide), BF16),
            pltpu.VMEM((CHUNKS, lanes, levels + 1, out_rows, 2 * wide), BF16),
            dma((5,)),
            dma((2,)),
            dma((len(ROUTES), PIECES)),
            dma((len(ROUTES), PIECES)),
            dma((FAR + 1,)),
            dma((FAR + 1,)),
            dma((2,)),
            dma((2,)),
            dma((CHUNKS,)),
            dma((CHUNKS,)),
            dma((CHUNKS, levels)),
            dma((CHUNKS, lanes, levels + 1)),
            dma((CHUNKS,)),
            pltpu.VMEM((CHUNKS, levels, out_rows, 2 * wide) if lanes == 2 else (1, 1, 8, 128), F32),
        ],
        compiler_params=pltpu.CompilerParams(
            collective_id=0, has_side_effects=True, vmem_limit_bytes=56 * 1024 * 1024
        ),
    )(green, direction, partners, counts)
    out = out.reshape(out_rows, half // 128, 2, 128)
    return jnp.swapaxes(out, 1, 2).reshape(out_rows, 2, half)


def solution(mesh):
    in_specs = (
        P(None, ("freq", "tile"), "src"),
        P(None, ("freq", "src"), None),
        P(("freq", "tile"), None),
        P(("freq", "tile")),
    )
    out_specs = P(("freq", "tile"), None, "src")
    body = functools.partial(shards, mesh.shape["tile"])
    return jax.shard_map(body, mesh=mesh, in_specs=in_specs, out_specs=out_specs, check_vma=False)
```

```python
import functools

import jax
import jax.numpy as jnp
from jax import lax
from jax.experimental import pallas as pl
from jax.experimental.pallas import tpu as pltpu
from jax.sharding import PartitionSpec as P

BAND_DEV = 3
PIECES = 8
CHUNKS = 4
OWN, ACROSS, NEAR, BACK, BACK_ACROSS, NEAR_ACROSS, FAR, PAIR, PAIR_ACROSS, PAIR_END, PAIR_END_ACROSS = range(11)
OFFSETS = (0, 1, 2, -2, -1, 3, -3)
ROUTES = (
    (OWN, ACROSS),
    (OWN, BACK),
    (OWN, NEAR),
    (ACROSS, NEAR_ACROSS),
    (NEAR, BACK_ACROSS),
    (BACK_ACROSS, FAR),
)
F32 = jnp.float32
BF16 = jnp.bfloat16


def dot(left, right, dims):
    return lax.dot_general(left, right, (dims, ((), ())), preferred_element_type=F32)


def short_line(out_rows, levels):
    return out_rows % 128 == 0 and levels <= 4


def kernel(
    count_tile, a_ref, v_ref, partners_ref, counts_ref, out_ref,
    table, sampled, win, vbuf, img, ipart, irecv, cpart, crecv, acc, w, turned, rr, hp, hr,
    load_sem, img_sem, route_send, route_recv, couple_send, couple_recv,
    pair_send, pair_recv, w_send, w_recv, h_send, h_recv, tot,
    gift, turned_end, rr_end, gift_send, gift_recv,
):
    me = lax.axis_index("tile")
    core = lax.axis_index("src")
    side = lax.rem(me, 2)
    level = me // 2
    levels = count_tile // 2
    step = 1 - 2 * side
    rows, half = win.shape[2], win.shape[3]
    tiles, kmax = table.shape
    out_rows = out_ref.shape[0]
    wide = half // CHUNKS

    def inside(place):
        return (place >= 0) & (place < levels)

    has_near = inside(level + step)
    has_back = inside(level - step)
    has_far = inside(level - 2 * step)
    across = {"tile": me + step}
    forward = {"tile": me + 2 * step}
    backward = {"tile": me - 2 * step}
    partner = {"src": 1 - core}
    targets = (across, forward, backward, backward, across, forward)
    sends = (None, has_near, has_back, has_back, has_near, has_near & has_back)
    arrives = (None, has_back, has_near, has_near, has_back, has_far)

    ends = short_line(out_rows, levels) and levels == 4
    last = CHUNKS - 1
    gives = (level == 0) | (level == levels - 1)
    takes = (level == 1) | (level == levels - 2)
    giver = jnp.where(level == 1, 0, levels - 1)
    end_near = giver == level + step
    end_slot = jnp.where(end_near, NEAR, BACK)
    end_across = jnp.where(end_near, NEAR_ACROSS, BACK_ACROSS)

    def guarded(condition, run):
        if condition is None:
            run()
        else:
            pl.when(condition)(run)

    def remote(source, target, send, recv, device):
        return pltpu.make_async_remote_copy(
            src_ref=source, dst_ref=target, send_sem=send, recv_sem=recv,
            device_id=device, device_id_type=pl.DeviceIdType.MESH,
        )

    def piece(slot, index):
        depth = 2 * rows // PIECES
        per = PIECES // 2
        return win.at[slot, index // per, pl.ds((index % per) * depth, depth)]

    def route(number, index):
        source, target = ROUTES[number]
        return remote(
            piece(source, index), piece(target, index),
            route_send.at[number, index], route_recv.at[number, index], targets[number],
        )

    def send_route(number, index):
        guarded(sends[number], lambda: route(number, index).start())

    def arrive(number, index):
        guarded(arrives[number], lambda: route(number, index).wait_recv())

    def to_pair(source, target, number):
        return remote(win.at[source], win.at[target], pair_send.at[number], pair_recv.at[number], partner)

    load_a = pltpu.make_async_copy(a_ref, win.at[OWN], load_sem.at[0])
    load_theirs = pltpu.make_async_copy(
        v_ref.at[:, :, pl.ds(pl.multiple_of((1 - core) * half, half), half)], vbuf.at[0], load_sem.at[1]
    )
    load_mine = pltpu.make_async_copy(
        v_ref.at[:, :, pl.ds(pl.multiple_of(core * half, half), half)], vbuf.at[1], load_sem.at[2]
    )
    load_table = pltpu.make_async_copy(partners_ref, table, load_sem.at[3])
    load_counts = pltpu.make_async_copy(counts_ref, sampled, load_sem.at[4])
    load_a.start()
    load_table.start()
    load_counts.start()
    load_theirs.start()
    load_mine.start()

    barrier = pltpu.get_barrier_semaphore()
    pl.semaphore_signal(barrier, inc=1, device_id=partner, device_id_type=pl.DeviceIdType.MESH)
    pl.semaphore_signal(barrier, inc=1, device_id=across, device_id_type=pl.DeviceIdType.MESH)

    def other_level(number):
        return lax.rem(level + 1 + number, levels)

    if short_line(out_rows, levels):
        for there, device in ((has_near, forward), (has_back, backward)):
            @pl.when(there)
            def _(device=device):
                pl.semaphore_signal(barrier, inc=1, device_id=device, device_id_type=pl.DeviceIdType.MESH)

        pl.semaphore_wait(barrier, 2 + has_near.astype(jnp.int32) + has_back.astype(jnp.int32))
    else:
        @pl.loop(0, levels - 1)
        def _(number):
            pl.semaphore_signal(
                barrier, inc=1, device_id={"tile": other_level(number) * 2 + side},
                device_id_type=pl.DeviceIdType.MESH,
            )

        pl.semaphore_wait(barrier, levels + 1)
    load_a.wait()
    for index in range(PIECES):
        for number in (0, 1, 2):
            send_route(number, index)
    to_pair(OWN, PAIR, 0).start()

    own = win[OWN].reshape(2 * rows, half)

    def images(slot):
        first = dot(own, vbuf[slot, 0], ((1,), (0,)))
        second = dot(own, vbuf[slot, 1], ((1,), (0,)))
        return first[:rows] - second[rows:], second[:rows] + first[rows:]

    load_theirs.wait()
    real, imag = images(0)
    ipart[0] = real
    ipart[1] = imag
    image_copy = remote(ipart, irecv, img_sem.at[0], img_sem.at[1], partner)
    image_copy.start()
    load_mine.wait()
    real, imag = images(1)
    image_copy.wait_recv()
    img[:rows] = (real + irecv[0]).astype(BF16)
    img[rows:] = (imag + irecv[1]).astype(BF16)

    load_table.wait()
    load_counts.wait()
    acc[...] = jnp.zeros_like(acc)

    def exists(slot):
        return (
            (slot <= ACROSS)
            | (((slot == NEAR) | (slot == NEAR_ACROSS)) & has_near)
            | (((slot == BACK) | (slot == BACK_ACROSS)) & has_back)
            | ((slot == FAR) & has_far)
        )

    def sample(slot):
        offset = 0
        for index, value in enumerate(OFFSETS):
            offset = jnp.where(slot == index, value, offset)
        first = (me + offset * step) * tiles
        tile = rows // tiles
        bands = []
        for row in range(tiles):
            blocks = []
            for column in range(tiles):
                hit = False
                for k in range(kmax):
                    hit = hit | ((table[row, k] == first + column) & (k < sampled[row]))
                blocks.append(jnp.full((tile, tile), jnp.where(hit, 1.0, 0.0), F32))
            bands.append(jnp.concatenate(blocks, axis=1))
        return jnp.concatenate(bands, axis=0)

    def couple_copy(slot):
        return remote(cpart.at[slot], crecv.at[slot], couple_send.at[slot], couple_recv.at[slot], partner)

    def couple(low, high):
        @pl.loop(low, high)
        def _(slot):
            @pl.when(exists(slot))
            def _():
                block = win[slot].reshape(2 * rows, half)
                prod = dot(img[...], block, ((1,), (1,)))
                cpart[slot, 0] = prod[:rows, :rows] + prod[rows:, rows:]
                cpart[slot, 1] = prod[rows:, :rows] - prod[:rows, rows:]
                couple_copy(slot).start()

    def weigh(low, high):
        @pl.loop(low, high)
        def _(slot):
            @pl.when(exists(slot))
            def _():
                couple_copy(slot).wait_recv()
                live = sample(slot)
                real = ((cpart[slot, 0] + crecv[slot, 0]) * live).astype(BF16)
                imag = ((cpart[slot, 1] + crecv[slot, 1]) * live).astype(BF16)
                left = jnp.concatenate(
                    [jnp.concatenate([real, -imag], axis=1), jnp.concatenate([imag, real], axis=1)], axis=0
                )
                acc[...] += dot(left, win[slot].reshape(2 * rows, half), ((1,), (0,)))

    def pass_on(index):
        arrive(0, index)
        send_route(3, index)
        arrive(2, index)
        send_route(4, index)

    couple(OWN, ACROSS)
    for index in range(PIECES):
        pass_on(index)
    to_pair(ACROSS, PAIR_ACROSS, 1).start()
    for index in range(PIECES):
        arrive(1, index)
    if ends:
        pl.when(takes)(lambda: to_pair(end_slot, PAIR_END, 2).start())
    span = max(out_rows, 128)

    def turn_over():
        to_pair(OWN, PAIR, 0).wait_recv()
        to_pair(ACROSS, PAIR_ACROSS, 1).wait_recv()

        @pl.loop(0, turned.shape[0])
        def _(group):
            column = (2 * group + side) * out_rows if span == out_rows else group * span
            which = column // half
            base = jnp.where(which == core, OWN, PAIR)
            lanes = pl.ds(pl.multiple_of(column - which * half, 128), span)
            for block in range(2):
                turned[group, :, block * 2 * rows : (block + 1) * 2 * rows] = (
                    win[base + block, :, :, lanes].reshape(2 * rows, span).T
                )

    jobs = (
        lambda: couple(ACROSS, BACK_ACROSS),
        lambda: weigh(OWN, NEAR),
        lambda: weigh(NEAR, BACK_ACROSS),
        turn_over,
    )
    for index in range(PIECES):
        for job in jobs[index * len(jobs) // PIECES : (index + 1) * len(jobs) // PIECES]:
            job()
        arrive(4, index)
        send_route(5, index)
    couple(BACK_ACROSS, NEAR_ACROSS)
    for index in range(PIECES):
        arrive(3, index)
    if ends:
        pl.when(takes)(lambda: to_pair(end_across, PAIR_END_ACROSS, 3).start())
    couple(NEAR_ACROSS, FAR)
    weigh(BACK_ACROSS, NEAR_ACROSS)
    for index in range(PIECES):
        arrive(5, index)
    couple(FAR, FAR + 1)
    weigh(NEAR_ACROSS, FAR + 1)

    def w_copy(chunk):
        return remote(w.at[chunk, 0], w.at[chunk, 1], w_send.at[chunk], w_recv.at[chunk], across)

    for chunk in range(CHUNKS):
        w[chunk, 0] = acc[:, chunk * wide : (chunk + 1) * wide].astype(BF16)
        w_copy(chunk).start()

    def gift_copy(hop):
        source = w.at[last, 0] if hop == 0 else gift.at[0]
        device = {"tile": me + jnp.where(level == 0, 2, -2)} if hop == 0 else across
        return remote(source, gift.at[hop], gift_send.at[hop], gift_recv.at[hop], device)

    if ends:
        pl.when(gives)(lambda: gift_copy(0).start())

        @pl.when(takes)
        def _():
            to_pair(end_slot, PAIR_END, 2).wait_recv()
            to_pair(end_across, PAIR_END_ACROSS, 3).wait_recv()
            for group in range(levels):
                column = (2 * group + side) * out_rows
                which = column // half
                lanes = pl.ds(pl.multiple_of(column - which * half, 128), span)
                for block, (here, there) in enumerate(((end_slot, PAIR_END), (end_across, PAIR_END_ACROSS))):
                    turned_end[group, :, block * 2 * rows : (block + 1) * 2 * rows] = (
                        win[jnp.where(which == core, here, there), :, :, lanes].reshape(2 * rows, span).T
                    )

    def partial(chunk, group):
        return dot(turned[group], rr[chunk], ((1,), (0,)))

    def rows_of(target):
        return pl.multiple_of((2 * target + side) * out_rows, out_rows)

    def spread(source, target, block):
        top, low = source[:rows], source[rows:]
        first = 2 * rows * block
        target[first : first + rows] = jnp.concatenate([top, low], axis=1)
        target[first + rows : first + 2 * rows] = jnp.concatenate([low, -top], axis=1)

    def prepare(chunk):
        for block in range(2):
            if block:
                w_copy(chunk).wait_recv()
            spread(w.at[chunk, block], rr.at[chunk], block)

    def put(chunk, total):
        for part in range(2):
            for index in range(wide // 128):
                first = part * wide + index * 128
                out_ref[:, 2 * (chunk * wide // 128 + index) + part] = total[:, first : first + 128]

    def term(chunk, lane, slot, target, level_to):
        return remote(
            hp.at[chunk, pl.ds(rows_of(target), out_rows)], hr.at[chunk, lane, slot],
            h_send.at[chunk, target], h_recv.at[chunk, lane, slot], {"tile": 2 * level_to + side},
        )

    if short_line(out_rows, levels):
        depths = level, levels - 1 - level

        def total(chunk):
            prepare(chunk)
            every = turned[...].reshape(levels * out_rows, 4 * rows)
            tot[chunk] = dot(every, rr[chunk], ((1,), (0,))).reshape(levels, out_rows, 2 * wide)

        def place(target):
            return pl.ds(rows_of(target), out_rows)

        def far(lane, number):
            return levels - 1 - number if lane == 0 else number

        def passing(chunk, lane, target):
            return term(chunk, lane, target, target, level + 1 - 2 * lane)

        def begin(chunk, numbers):
            for lane in range(2):
                for number in numbers:
                    target = far(lane, number)

                    @pl.when(depths[lane] == 0)
                    def _(lane=lane, target=target):
                        hp[chunk, place(target)] = tot[chunk, target].astype(BF16)
                        passing(chunk, lane, target).start()

        def beside(chunk):
            for lane in range(2):
                target = far(lane, 0)

                @pl.when(depths[lane] == 2)
                def _(lane=lane, target=target):
                    hp[chunk, place(target)] = tot[chunk, target].astype(BF16)
                    term(chunk, lane, levels, target, target).start()

        def add_on(chunk, number):
            for lane in range(2):
                target = far(lane, number)

                @pl.when(depths[lane] == 1)
                def _(lane=lane, target=target):
                    value = tot[chunk, target]
                    if not (ends and chunk == last):
                        passing(chunk, lane, target).wait_recv()
                        value = value + hr[chunk, lane, target].astype(F32)
                    hp[chunk, place(target)] = value.astype(BF16)
                    term(chunk, lane, target, target, target).start()

        def pass_gift():
            @pl.when(takes)
            def _():
                gift_copy(0).wait_recv()
                gift_copy(1).start()

        def use_gift():
            @pl.when(takes)
            def _():
                gift_copy(1).wait_recv()
                for block in range(2):
                    spread(gift.at[block], rr_end, block)
                every = turned_end[...].reshape(levels * out_rows, 4 * rows)
                more = dot(every, rr_end[...], ((1,), (0,))).reshape(levels, out_rows, 2 * wide)
                for target in range(1, levels - 1):
                    tot[last, target] += more[target]
                far_end = jnp.where(level == 1, levels - 1, 0)
                tot[last, far_end] += jnp.where(level == 1, more[levels - 1], more[0])

        distant = range(levels - 2)

        given = CHUNKS - 1 if ends else CHUNKS
        for chunk in range(CHUNKS + 1):
            if chunk < CHUNKS:
                total(chunk)
                if chunk < given:
                    begin(chunk, distant)
                if levels > 3:
                    beside(chunk)
            if chunk == given - 1 and levels > 1:
                for done in range(given):
                    begin(done, (levels - 2,))
            if ends and chunk == 0:
                pass_gift()
            if ends and chunk == CHUNKS:
                use_gift()
            for number in distant:
                if 0 <= chunk - 1 < CHUNKS:
                    add_on(chunk - 1, number)

        for chunk in range(CHUNKS):
            for lane, slot, there in (
                (0, level, depths[0] > 0), (1, level, depths[1] > 0),
                (0, levels, depths[0] > 2), (1, levels, depths[1] > 2),
            ):
                if ends and chunk == last and slot is level:
                    there = depths[lane] > 1

                @pl.when(there)
                def _(chunk=chunk, lane=lane, slot=slot):
                    term(chunk, lane, slot, level, level).wait_recv()
                    tot[chunk, level] += hr[chunk, lane, slot].astype(F32)
            put(chunk, tot[chunk, level])
    else:
        for chunk in range(CHUNKS):
            prepare(chunk)
            if span != out_rows:
                @pl.loop(0, hp.shape[1] // span)
                def _(group):
                    column = pl.multiple_of(group * span, span)
                    hp[chunk, pl.ds(column, span)] = partial(chunk, group).astype(BF16)

            @pl.loop(0, levels - 1)
            def _(number):
                target = other_level(number)
                if span == out_rows:
                    hp[chunk, pl.ds(rows_of(target), out_rows)] = partial(chunk, target).astype(BF16)
                term(chunk, 0, level, target, target).start()

            if span == out_rows:
                hp[chunk, pl.ds(rows_of(level), out_rows)] = partial(chunk, level).astype(BF16)

        for chunk in range(CHUNKS):
            def add(number, total):
                sender = other_level(number)
                term(chunk, 0, sender, level, sender).wait_recv()
                return total + hr[chunk, 0, sender].astype(F32)

            put(chunk, lax.fori_loop(0, levels - 1, add, hp[chunk, pl.ds(rows_of(level), out_rows)].astype(F32)))

    for number in range(len(ROUTES)):
        for index in range(PIECES):
            guarded(sends[number], lambda number=number, index=index: route(number, index).wait_send())
    to_pair(OWN, PAIR, 0).wait_send()
    to_pair(ACROSS, PAIR_ACROSS, 1).wait_send()
    image_copy.wait_send()

    @pl.loop(0, FAR + 1)
    def _(slot):
        @pl.when(exists(slot))
        def _():
            couple_copy(slot).wait_send()

    if ends:
        pl.when(gives)(lambda: gift_copy(0).wait_send())

        @pl.when(takes)
        def _():
            gift_copy(1).wait_send()
            to_pair(end_slot, PAIR_END, 2).wait_send()
            to_pair(end_across, PAIR_END_ACROSS, 3).wait_send()

    for chunk in range(CHUNKS):
        w_copy(chunk).wait_send()

        @pl.loop(0, jnp.where(gives, 0, levels - 1) if ends and chunk == last else levels - 1)
        def _(number):
            target = other_level(number)
            term(chunk, 0, target, target, target).wait_send()


def shards(count_tile, green, direction, partners, counts):
    tile_dev, kmax = partners.shape
    rows, half = green.shape[1:]
    sources = direction.shape[2]
    out_rows = sources // count_tile
    levels = count_tile // 2
    wide = half // CHUNKS
    lanes = 2 if short_line(out_rows, levels) else 1
    anywhere = pl.BlockSpec(memory_space=pl.ANY)
    local = pl.BlockSpec(memory_space=pltpu.VMEM)
    dma = pltpu.SemaphoreType.DMA
    out = pl.pallas_call(
        functools.partial(kernel, count_tile),
        out_shape=jax.ShapeDtypeStruct((out_rows, half // 64, 128), F32),
        in_specs=[anywhere] * 4,
        out_specs=local,
        scratch_shapes=[
            pltpu.SMEM((tile_dev, kmax), jnp.int32),
            pltpu.SMEM((tile_dev,), jnp.int32),
            pltpu.VMEM((PAIR_END_ACROSS + 1, 2, rows, half), BF16),
            pltpu.VMEM((2, 2, half, half), BF16),
            pltpu.VMEM((2 * rows, half), BF16),
            pltpu.VMEM((2, rows, half), F32),
            pltpu.VMEM((2, rows, half), F32),
            pltpu.VMEM((FAR + 1, 2, rows, rows), F32),
            pltpu.VMEM((FAR + 1, 2, rows, rows), F32),
            pltpu.VMEM((2 * rows, half), F32),
            pltpu.VMEM((CHUNKS, 2, 2 * rows, wide), BF16),
            pltpu.VMEM((levels if out_rows >= 128 else sources // 128, max(out_rows, 128), 4 * rows), BF16),
            pltpu.VMEM((CHUNKS, 4 * rows, 2 * wide), BF16),
            pltpu.VMEM((CHUNKS, sources, 2 * wide), BF16),
            pltpu.VMEM((CHUNKS, lanes, levels + 1, out_rows, 2 * wide), BF16),
            dma((5,)),
            dma((2,)),
            dma((len(ROUTES), PIECES)),
            dma((len(ROUTES), PIECES)),
            dma((FAR + 1,)),
            dma((FAR + 1,)),
            dma((4,)),
            dma((4,)),
            dma((CHUNKS,)),
            dma((CHUNKS,)),
            dma((CHUNKS, levels)),
            dma((CHUNKS, lanes, levels + 1)),
            pltpu.VMEM((CHUNKS, levels, out_rows, 2 * wide) if lanes == 2 else (1, 1, 8, 128), F32),
            pltpu.VMEM((2, 2 * rows, wide), BF16),
            pltpu.VMEM((levels, out_rows, 4 * rows) if lanes == 2 else (1, 16, 128), BF16),
            pltpu.VMEM((4 * rows, 2 * wide), BF16),
            dma((2,)),
            dma((2,)),
        ],
        compiler_params=pltpu.CompilerParams(
            collective_id=0, has_side_effects=True, vmem_limit_bytes=56 * 1024 * 1024
        ),
    )(green, direction, partners, counts)
    out = out.reshape(out_rows, half // 128, 2, 128)
    return jnp.swapaxes(out, 1, 2).reshape(out_rows, 2, half)


def solution(mesh):
    in_specs = (
        P(None, ("freq", "tile"), "src"),
        P(None, ("freq", "src"), None),
        P(("freq", "tile"), None),
        P(("freq", "tile")),
    )
    out_specs = P(("freq", "tile"), None, "src")
    body = functools.partial(shards, mesh.shape["tile"])
    return jax.shard_map(body, mesh=mesh, in_specs=in_specs, out_specs=out_specs, check_vma=False)
```

```python
import functools

import jax
import jax.numpy as jnp
from jax import lax
from jax.experimental import pallas as pl
from jax.experimental.pallas import tpu as pltpu
from jax.sharding import PartitionSpec as P

BAND_DEV = 3
PIECES = 8
CHUNKS = 4
SHORT_CHUNKS = 8
GIFTS = 1
PASS_AT = 4
GIVE_AT = 1
OWN, ACROSS, NEAR, BACK, BACK_ACROSS, NEAR_ACROSS, FAR, PAIR, PAIR_ACROSS, PAIR_END, PAIR_END_ACROSS = range(11)
OFFSETS = (0, 1, 2, -2, -1, 3, -3)
ROUTES = (
    (OWN, ACROSS),
    (OWN, BACK),
    (OWN, NEAR),
    (ACROSS, NEAR_ACROSS),
    (NEAR, BACK_ACROSS),
    (BACK_ACROSS, FAR),
)
RELAYED = (0, 2, 4)
F32 = jnp.float32
BF16 = jnp.bfloat16


def dot(left, right, dims):
    return lax.dot_general(left, right, (dims, ((), ())), preferred_element_type=F32)


def short_line(out_rows, levels):
    return out_rows % 128 == 0 and levels <= 4


def kernel(
    count_tile, a_ref, v_ref, partners_ref, counts_ref, out_ref,
    table, sampled, win, vbuf, img, ipart, irecv, cpart, crecv, acc, w, turned, hp, hr,
    load_sem, img_sem, route_send, relay_recv, final_recv, couple_send, couple_recv,
    pair_send, pair_recv, w_send, w_recv, h_send, h_recv, tot,
    gift, turned_end, gift_send, gift_recv, far_sums,
):
    me = lax.axis_index("tile")
    core = lax.axis_index("src")
    side = lax.rem(me, 2)
    level = me // 2
    levels = count_tile // 2
    step = 1 - 2 * side
    rows, half = win.shape[2], win.shape[3]
    tiles, kmax = table.shape
    out_rows = out_ref.shape[0]
    chunks, wide = w.shape[0], w.shape[3] // 2

    def inside(place):
        return (place >= 0) & (place < levels)

    has_near = inside(level + step)
    has_back = inside(level - step)
    has_far = inside(level - 2 * step)
    across = {"tile": me + step}
    forward = {"tile": me + 2 * step}
    backward = {"tile": me - 2 * step}
    partner = {"src": 1 - core}
    targets = (across, forward, backward, backward, across, forward)
    sends = (None, has_near, has_back, has_back, has_near, has_near & has_back)
    arrives = (None, has_back, has_near, has_near, has_back, has_far)

    ends = short_line(out_rows, levels) and levels == 4
    given = chunks - gift.shape[0] if ends else chunks
    gives = (level == 0) | (level == levels - 1)
    takes = (level == 1) | (level == levels - 2)
    giver = jnp.where(level == 1, 0, levels - 1)
    end_near = giver == level + step
    end_slot = jnp.where(end_near, NEAR, BACK)
    end_across = jnp.where(end_near, NEAR_ACROSS, BACK_ACROSS)

    def guarded(condition, run):
        if condition is None:
            run()
        else:
            pl.when(condition)(run)

    def remote(source, target, send, recv, device):
        return pltpu.make_async_remote_copy(
            src_ref=source, dst_ref=target, send_sem=send, recv_sem=recv,
            device_id=device, device_id_type=pl.DeviceIdType.MESH,
        )

    depth = rows // PIECES
    parts = 2 if rows % 256 == 0 else 1

    def piece(slot, index, count=1):
        return win.at[slot, :, pl.ds(index * depth, count * depth)]

    def route(number, index, count=1):
        source, target = ROUTES[number]
        if number in RELAYED:
            recv = relay_recv.at[RELAYED.index(number), index]
        else:
            recv = final_recv.at[number, index * parts // PIECES if number == 5 else 0]
        return remote(
            piece(source, index, count), piece(target, index, count), route_send.at[number], recv, targets[number]
        )

    def send_route(number, index):
        guarded(sends[number], lambda: route(number, index).start())

    def arrive(number, index, count=1):
        guarded(arrives[number], lambda: route(number, index, count).wait_recv())

    def to_pair(source, target, number):
        return remote(win.at[source], win.at[target], pair_send.at[number], pair_recv.at[number], partner)

    load_a = pltpu.make_async_copy(a_ref, win.at[OWN], load_sem.at[0])
    load_theirs = pltpu.make_async_copy(
        v_ref.at[:, :, pl.ds(pl.multiple_of((1 - core) * half, half), half)], vbuf.at[0], load_sem.at[1]
    )
    load_mine = pltpu.make_async_copy(
        v_ref.at[:, :, pl.ds(pl.multiple_of(core * half, half), half)], vbuf.at[1], load_sem.at[2]
    )
    load_table = pltpu.make_async_copy(partners_ref, table, load_sem.at[3])
    load_counts = pltpu.make_async_copy(counts_ref, sampled, load_sem.at[4])
    load_a.start()
    load_table.start()
    load_counts.start()
    load_theirs.start()
    load_mine.start()

    barrier = pltpu.get_barrier_semaphore()
    pl.semaphore_signal(barrier, inc=1, device_id=partner, device_id_type=pl.DeviceIdType.MESH)
    pl.semaphore_signal(barrier, inc=1, device_id=across, device_id_type=pl.DeviceIdType.MESH)

    def other_level(number):
        return lax.rem(level + 1 + number, levels)

    if short_line(out_rows, levels):
        for there, device in ((has_near, forward), (has_back, backward)):
            @pl.when(there)
            def _(device=device):
                pl.semaphore_signal(barrier, inc=1, device_id=device, device_id_type=pl.DeviceIdType.MESH)

        pl.semaphore_wait(barrier, 2 + has_near.astype(jnp.int32) + has_back.astype(jnp.int32))
    else:
        @pl.loop(0, levels - 1)
        def _(number):
            pl.semaphore_signal(
                barrier, inc=1, device_id={"tile": other_level(number) * 2 + side},
                device_id_type=pl.DeviceIdType.MESH,
            )

        pl.semaphore_wait(barrier, levels + 1)
    load_a.wait()
    for index in range(PIECES):
        for number in (0, 1, 2):
            send_route(number, index)
    to_pair(OWN, PAIR, 0).start()

    own = win[OWN].reshape(2 * rows, half)

    def images(slot):
        first = dot(own, vbuf[slot, 0], ((1,), (0,)))
        second = dot(own, vbuf[slot, 1], ((1,), (0,)))
        return first[:rows] - second[rows:], second[:rows] + first[rows:]

    load_theirs.wait()
    real, imag = images(0)
    ipart[0] = real
    ipart[1] = imag
    image_copy = remote(ipart, irecv, img_sem.at[0], img_sem.at[1], partner)
    image_copy.start()
    load_mine.wait()
    real, imag = images(1)
    image_copy.wait_recv()
    img[:rows] = (real + irecv[0]).astype(BF16)
    img[rows:] = (imag + irecv[1]).astype(BF16)

    load_table.wait()
    load_counts.wait()
    acc[...] = jnp.zeros_like(acc)

    def exists(slot):
        return (
            (slot <= ACROSS)
            | (((slot == NEAR) | (slot == NEAR_ACROSS)) & has_near)
            | (((slot == BACK) | (slot == BACK_ACROSS)) & has_back)
            | ((slot == FAR) & has_far)
        )

    def sample(slot):
        offset = 0
        for index, value in enumerate(OFFSETS):
            offset = jnp.where(slot == index, value, offset)
        first = (me + offset * step) * tiles
        tile = rows // tiles
        bands = []
        for row in range(tiles):
            blocks = []
            for column in range(tiles):
                hit = False
                for k in range(kmax):
                    hit = hit | ((table[row, k] == first + column) & (k < sampled[row]))
                blocks.append(jnp.full((tile, tile), jnp.where(hit, 1.0, 0.0), F32))
            bands.append(jnp.concatenate(blocks, axis=1))
        return jnp.concatenate(bands, axis=0)

    def couple_copy(slot):
        return remote(cpart.at[slot], crecv.at[slot], couple_send.at[slot], couple_recv.at[slot], partner)

    def couple(low, high):
        @pl.loop(low, high)
        def _(slot):
            @pl.when(exists(slot))
            def _():
                block = win[slot].reshape(2 * rows, half)
                prod = dot(img[...], block, ((1,), (1,)))
                cpart[slot, 0] = prod[:rows, :rows] + prod[rows:, rows:]
                cpart[slot, 1] = prod[rows:, :rows] - prod[:rows, rows:]
                couple_copy(slot).start()

    def weigh(low, high):
        @pl.loop(low, high)
        def _(slot):
            @pl.when(exists(slot))
            def _():
                couple_copy(slot).wait_recv()
                live = sample(slot)
                real = ((cpart[slot, 0] + crecv[slot, 0]) * live).astype(BF16)
                imag = ((cpart[slot, 1] + crecv[slot, 1]) * live).astype(BF16)
                left = jnp.concatenate(
                    [jnp.concatenate([real, -imag], axis=1), jnp.concatenate([imag, real], axis=1)], axis=0
                )
                acc[...] += dot(left, win[slot].reshape(2 * rows, half), ((1,), (0,)))

    def pass_on(index):
        arrive(0, index)
        send_route(3, index)
        arrive(2, index)
        send_route(4, index)

    couple(OWN, ACROSS)
    for index in range(PIECES):
        pass_on(index)
    to_pair(ACROSS, PAIR_ACROSS, 1).start()
    arrive(1, 0, PIECES)
    if ends:
        pl.when(takes)(lambda: to_pair(end_slot, PAIR_END, 2).start())
    span = max(out_rows, 128)

    def lay(target, group, block, slot, lanes):
        for part in range(2):
            first = (2 * part + block) * rows
            target[group, :, first : first + rows] = win[slot, part, :, lanes].T

    def turn_over():
        to_pair(OWN, PAIR, 0).wait_recv()
        to_pair(ACROSS, PAIR_ACROSS, 1).wait_recv()

        @pl.loop(0, turned.shape[0])
        def _(group):
            column = (2 * group + side) * out_rows if span == out_rows else group * span
            which = column // half
            base = jnp.where(which == core, OWN, PAIR)
            lanes = pl.ds(pl.multiple_of(column - which * half, 128), span)
            for block in range(2):
                lay(turned, group, block, base + block, lanes)

    jobs = (
        lambda: couple(ACROSS, BACK_ACROSS),
        lambda: weigh(OWN, NEAR),
        lambda: weigh(NEAR, BACK_ACROSS),
        turn_over,
    )
    for index in range(PIECES):
        for job in jobs[index * len(jobs) // PIECES : (index + 1) * len(jobs) // PIECES]:
            job()
        arrive(4, index)
        send_route(5, index)
    couple(BACK_ACROSS, NEAR_ACROSS)
    arrive(3, 0, PIECES)
    if ends:
        pl.when(takes)(lambda: to_pair(end_across, PAIR_END_ACROSS, 3).start())
    couple(NEAR_ACROSS, FAR)
    weigh(BACK_ACROSS, NEAR_ACROSS)
    part_rows = rows // parts

    def far_part(part):
        return win[FAR, :, part * part_rows : (part + 1) * part_rows].reshape(2 * part_rows, half)

    def far_copy(part):
        return remote(
            far_sums.at[0, part], far_sums.at[1, part],
            couple_send.at[FAR + part], couple_recv.at[FAR + part], partner,
        )

    def couple_far(part):
        @pl.when(has_far)
        def _():
            arrive_far(part)
            prod = dot(img[...], far_part(part), ((1,), (1,)))
            for index, value in enumerate((
                prod[:rows, :part_rows] + prod[rows:, part_rows:],
                prod[rows:, :part_rows] - prod[:rows, part_rows:],
            )):
                far_sums[0, part, index] = value
            far_copy(part).start()

    def arrive_far(part):
        route(5, part * PIECES // parts, PIECES // parts).wait_recv()

    def weigh_far(part):
        @pl.when(has_far)
        def _():
            far_copy(part).wait_recv()
            columns = slice(part * part_rows, (part + 1) * part_rows)
            live = sample(FAR)[:, columns]
            real = ((far_sums[0, part, 0] + far_sums[1, part, 0]) * live).astype(BF16)
            imag = ((far_sums[0, part, 1] + far_sums[1, part, 1]) * live).astype(BF16)
            left = jnp.concatenate(
                [jnp.concatenate([real, -imag], axis=1), jnp.concatenate([imag, real], axis=1)], axis=0
            )
            acc[...] += dot(left, far_part(part), ((1,), (0,)))

    weigh(NEAR_ACROSS, FAR)
    for part in range(parts):
        couple_far(part)
        if part:
            weigh_far(part - 1)
    weigh_far(parts - 1)

    def w_copy(chunk):
        return remote(w.at[chunk, 0], w.at[chunk, 1], w_send.at[0], w_recv.at[chunk], across)

    def halves(first, second):
        low = lax.broadcasted_iota(jnp.int32, first.shape, 1) < wide
        return (
            jnp.where(low, first, pltpu.roll(second, wide, 1)),
            jnp.where(low, pltpu.roll(first, wide, 1), second),
        )

    def gift_copy(index, hop):
        source = w.at[given + index, 0] if hop == 0 else gift.at[index, 0]
        device = {"tile": me + jnp.where(level == 0, 2, -2)} if hop == 0 else across
        return remote(
            source, gift.at[index, hop], gift_send.at[index, hop], gift_recv.at[index, hop], device
        )

    span_chunks = 2 if wide % 128 else 1
    for first in range(0, chunks, span_chunks):
        columns = slice(first * wide, (first + span_chunks) * wide)
        real, imag = acc[:rows, columns], acc[rows:, columns]
        if wide % 128:
            packed = halves(real, imag)
        else:
            packed = (jnp.concatenate([real, imag], axis=1),)
        for index, value in enumerate(packed):
            w[first + index, 0] = value.astype(BF16)
            w_copy(first + index).start()

    def give(when):
        @pl.when(gives & when)
        def _():
            for index in range(chunks - given):
                gift_copy(index, 0).start()

    if ends:
        give(jnp.logical_not(has_far))

        @pl.when(takes)
        def _():
            to_pair(end_slot, PAIR_END, 2).wait_recv()
            to_pair(end_across, PAIR_END_ACROSS, 3).wait_recv()
            for group in range(levels):
                column = (2 * group + side) * out_rows
                which = column // half
                lanes = pl.ds(pl.multiple_of(column - which * half, 128), span)
                for block, (here, there) in enumerate(((end_slot, PAIR_END), (end_across, PAIR_END_ACROSS))):
                    lay(turned_end, group, block, jnp.where(which == core, here, there), lanes)

    def product(left, right):
        straight = dot(left[:, : 2 * rows], right, ((1,), (0,)))
        crossed = pltpu.roll(dot(left[:, 2 * rows :], right, ((1,), (0,))), wide, 1)
        low = lax.broadcasted_iota(jnp.int32, crossed.shape, 1) < wide
        return straight + jnp.where(low, crossed, -crossed)

    def partial(chunk, group):
        return product(turned[group], w[chunk].reshape(2 * rows, 2 * wide))

    def rows_of(target):
        return pl.multiple_of((2 * target + side) * out_rows, out_rows)

    def put(chunk, total):
        for part in range(2):
            for index in range(wide // 128):
                first = part * wide + index * 128
                out_ref[:, 2 * (chunk * wide // 128 + index) + part] = total[:, first : first + 128]

    def term(chunk, lane, slot, target, level_to, arrival=None):
        return remote(
            hp.at[chunk, pl.ds(rows_of(target), out_rows)], hr.at[chunk, lane, slot],
            h_send.at[0], h_recv.at[chunk, slot if arrival is None else arrival], {"tile": 2 * level_to + side},
        )

    def settle():
        for number in range(len(ROUTES)):
            guarded(sends[number], lambda number=number: route(number, 0, PIECES).wait_send())
        to_pair(OWN, PAIR, 0).wait_send()
        to_pair(ACROSS, PAIR_ACROSS, 1).wait_send()
        image_copy.wait_send()

        @pl.loop(0, FAR)
        def _(slot):
            @pl.when(exists(slot))
            def _():
                couple_copy(slot).wait_send()

        @pl.when(has_far)
        def _():
            for part in range(parts):
                far_copy(part).wait_send()

        if ends:
            @pl.when(gives)
            def _():
                for index in range(chunks - given):
                    gift_copy(index, 0).wait_send()

            @pl.when(takes)
            def _():
                for index in range(chunks - given):
                    gift_copy(index, 1).wait_send()
                to_pair(end_slot, PAIR_END, 2).wait_send()
                to_pair(end_across, PAIR_END_ACROSS, 3).wait_send()

        remote(w.at[:, 0], w.at[:, 1], w_send.at[0], w_recv.at[0], across).wait_send()

        def sent(count):
            rows_sent = hp.at[:count, pl.ds(0, (levels - 1) * out_rows)]
            remote(rows_sent, rows_sent, h_send.at[0], h_recv.at[0, 0], across).wait_send()

        if levels > 1:
            if given == chunks:
                sent(chunks)
            else:
                pl.when(gives)(lambda: sent(given))
                pl.when(takes)(lambda: sent(chunks))

    if short_line(out_rows, levels):
        depths = level, levels - 1 - level

        def total(chunk):
            w_copy(chunk).wait_recv()
            every = turned[...].reshape(levels * out_rows, 4 * rows)
            tot[chunk] = product(every, w[chunk].reshape(2 * rows, 2 * wide)).reshape(levels, out_rows, 2 * wide)

        def place(target):
            return pl.ds(rows_of(target), out_rows)

        def far(lane, number):
            return levels - 1 - number if lane == 0 else number

        def passing(chunk, lane, target, number):
            arrival = number if number < levels - 2 else 2 + lane
            return term(chunk, lane, target, target, level + 1 - 2 * lane, arrival)

        def begin(chunk, numbers):
            for lane in range(2):
                for number in numbers:
                    target = far(lane, number)

                    @pl.when(depths[lane] == 0)
                    def _(lane=lane, target=target, number=number):
                        hp[chunk, place(target)] = tot[chunk, target].astype(BF16)
                        passing(chunk, lane, target, number).start()

        def beside(chunk):
            for lane in range(2):
                target = far(lane, 0)

                @pl.when(depths[lane] == 2)
                def _(lane=lane, target=target):
                    hp[chunk, place(target)] = tot[chunk, target].astype(BF16)
                    term(chunk, lane, levels, target, target, 0).start()

        def add_on(chunk, number):
            for lane in range(2):
                target = far(lane, number)

                @pl.when(depths[lane] == 1)
                def _(lane=lane, target=target):
                    value = tot[chunk, target]
                    if chunk < given:
                        passing(chunk, lane, target, number).wait_recv()
                        value = value + hr[chunk, lane, target].astype(F32)
                    hp[chunk, place(target)] = value.astype(BF16)
                    term(chunk, lane, target, target, target, 2 + lane).start()

        def pass_gift(index):
            @pl.when(takes)
            def _():
                gift_copy(index, 0).wait_recv()
                gift_copy(index, 1).start()

        def use_gift(index):
            @pl.when(takes)
            def _():
                gift_copy(index, 1).wait_recv()
                every = turned_end[...].reshape(levels * out_rows, 4 * rows)
                more = product(every, gift[index].reshape(2 * rows, 2 * wide)).reshape(levels, out_rows, 2 * wide)
                for target in range(1, levels - 1):
                    tot[given + index, target] += more[target]
                far_end = jnp.where(level == 1, levels - 1, 0)
                tot[given + index, far_end] += jnp.where(level == 1, more[levels - 1], more[0])

        distant = range(levels - 2)

        for chunk in range(chunks + 1):
            if chunk < chunks:
                total(chunk)
                if chunk < given:
                    begin(chunk, distant)
                if levels > 3:
                    beside(chunk)
            if ends and chunk == GIVE_AT:
                give(has_far)
            if chunk == given - 1 and levels > 1:
                for done in range(given):
                    begin(done, (levels - 2,))
            if 0 <= chunk - PASS_AT < chunks - given:
                pass_gift(chunk - PASS_AT)
            if chunk > given:
                use_gift(chunk - 1 - given)
            if chunk > 0:
                for number in distant:
                    add_on(chunk - 1, number)

        for chunk in range(chunks):
            if chunk == chunks - 1:
                settle()
            for lane, slot, arrival, there in (
                (0, level, 2, depths[0] > (1 if chunk >= given else 0)),
                (1, level, 3, depths[1] > (1 if chunk >= given else 0)),
                (0, levels, 0, depths[0] > 2), (1, levels, 0, depths[1] > 2),
            ):
                @pl.when(there)
                def _(chunk=chunk, lane=lane, slot=slot, arrival=arrival):
                    term(chunk, lane, slot, level, level, arrival).wait_recv()
                    tot[chunk, level] += hr[chunk, lane, slot].astype(F32)
            if wide % 128 == 0:
                put(chunk, tot[chunk, level])
            elif chunk % 2:
                for part, value in enumerate(halves(tot[chunk - 1, level], tot[chunk, level])):
                    out_ref[:, chunk - 1 + part] = value
    else:
        for chunk in range(chunks):
            w_copy(chunk).wait_recv()
            if span != out_rows:
                @pl.loop(0, hp.shape[1] // span)
                def _(group):
                    column = pl.multiple_of(group * span, span)
                    hp[chunk, pl.ds(column, span)] = partial(chunk, group).astype(BF16)

            @pl.loop(0, levels - 1)
            def _(number):
                target = other_level(number)
                if span == out_rows:
                    hp[chunk, pl.ds(rows_of(target), out_rows)] = partial(chunk, target).astype(BF16)
                term(chunk, 0, level, target, target).start()

            if span == out_rows:
                hp[chunk, pl.ds(rows_of(level), out_rows)] = partial(chunk, level).astype(BF16)

        for chunk in range(chunks):
            def add(number, total):
                sender = other_level(number)
                term(chunk, 0, sender, level, sender).wait_recv()
                return total + hr[chunk, 0, sender].astype(F32)

            put(chunk, lax.fori_loop(0, levels - 1, add, hp[chunk, pl.ds(rows_of(level), out_rows)].astype(F32)))

        settle()

def shards(count_tile, green, direction, partners, counts):
    tile_dev, kmax = partners.shape
    rows, half = green.shape[1:]
    sources = direction.shape[2]
    out_rows = sources // count_tile
    levels = count_tile // 2
    chunks = SHORT_CHUNKS if short_line(out_rows, levels) else CHUNKS
    wide = half // chunks
    parts = 2 if rows % 256 == 0 else 1
    lanes = 2 if short_line(out_rows, levels) else 1
    anywhere = pl.BlockSpec(memory_space=pl.ANY)
    local = pl.BlockSpec(memory_space=pltpu.VMEM)
    dma = pltpu.SemaphoreType.DMA
    out = pl.pallas_call(
        functools.partial(kernel, count_tile),
        out_shape=jax.ShapeDtypeStruct((out_rows, half // 64, 128), F32),
        in_specs=[anywhere] * 4,
        out_specs=local,
        scratch_shapes=[
            pltpu.SMEM((tile_dev, kmax), jnp.int32),
            pltpu.SMEM((tile_dev,), jnp.int32),
            pltpu.VMEM((PAIR_END_ACROSS + 1, 2, rows, half), BF16),
            pltpu.VMEM((2, 2, half, half), BF16),
            pltpu.VMEM((2 * rows, half), BF16),
            pltpu.VMEM((2, rows, half), F32),
            pltpu.VMEM((2, rows, half), F32),
            pltpu.VMEM((FAR, 2, rows, rows), F32),
            pltpu.VMEM((FAR, 2, rows, rows), F32),
            pltpu.VMEM((2 * rows, half), F32),
            pltpu.VMEM((chunks, 2, rows, 2 * wide), BF16),
            pltpu.VMEM((levels if out_rows >= 128 else sources // 128, max(out_rows, 128), 4 * rows), BF16),
            pltpu.VMEM((chunks, sources, 2 * wide), BF16),
            pltpu.VMEM((chunks, lanes, levels + 1, out_rows, 2 * wide), BF16),
            dma((5,)),
            dma((2,)),
            dma((len(ROUTES),)),
            dma((len(RELAYED), PIECES)),
            dma((len(ROUTES), 2)),
            dma((FAR + 2,)),
            dma((FAR + 2,)),
            dma((4,)),
            dma((4,)),
            dma((1,)),
            dma((chunks,)),
            dma((1,)),
            dma((chunks, 4 if lanes == 2 else levels + 1)),
            pltpu.VMEM((chunks, levels, out_rows, 2 * wide) if lanes == 2 else (1, 1, 8, 128), F32),
            pltpu.VMEM((GIFTS, 2, rows, 2 * wide), BF16),
            pltpu.VMEM((levels, out_rows, 4 * rows) if lanes == 2 else (1, 16, 128), BF16),
            dma((GIFTS, 2)),
            dma((GIFTS, 2)),
            pltpu.VMEM((2, parts, 2, rows, rows // parts), F32),
        ],
        compiler_params=pltpu.CompilerParams(
            collective_id=0, has_side_effects=True, vmem_limit_bytes=56 * 1024 * 1024
        ),
    )(green, direction, partners, counts)
    out = out.reshape(out_rows, half // 128, 2, 128)
    return jnp.swapaxes(out, 1, 2).reshape(out_rows, 2, half)


def solution(mesh):
    in_specs = (
        P(None, ("freq", "tile"), "src"),
        P(None, ("freq", "src"), None),
        P(("freq", "tile"), None),
        P(("freq", "tile")),
    )
    out_specs = P(("freq", "tile"), None, "src")
    body = functools.partial(shards, mesh.shape["tile"])
    return jax.shard_map(body, mesh=mesh, in_specs=in_specs, out_specs=out_specs, check_vma=False)
```

```python
import functools

import jax
import jax.numpy as jnp
from jax import lax
from jax.experimental import pallas as pl
from jax.experimental.pallas import tpu as pltpu
from jax.sharding import PartitionSpec as P

BAND_DEV = 3
PIECES = 8
CHUNKS = 4
SHORT_CHUNKS = 8
GIFTS = 1
PASS_AT = 3
TURN_AT = 4
GIVE_AT = 1
OWN, ACROSS, NEAR, BACK, BACK_ACROSS, NEAR_ACROSS, FAR, PAIR, PAIR_ACROSS, PAIR_END, PAIR_END_ACROSS = range(11)
OFFSETS = (0, 1, 2, -2, -1, 3, -3)
ROUTES = (
    (OWN, ACROSS),
    (OWN, BACK),
    (OWN, NEAR),
    (ACROSS, NEAR_ACROSS),
    (NEAR, BACK_ACROSS),
    (BACK_ACROSS, FAR),
)
RELAYED = (0, 2, 4)
F32 = jnp.float32
BF16 = jnp.bfloat16


def dot(left, right, dims):
    return lax.dot_general(left, right, (dims, ((), ())), preferred_element_type=F32)


def short_line(out_rows, levels):
    return out_rows % 128 == 0 and levels <= 4


def kernel(
    count_tile, a_ref, v_ref, partners_ref, counts_ref, out_ref,
    table, sampled, win, vbuf, img, ipart, irecv, cpart, crecv, acc, w, turned, hp, hr,
    load_sem, img_sem, route_send, relay_recv, final_recv, couple_send, couple_recv,
    pair_send, pair_recv, w_send, w_recv, h_send, h_recv, tot,
    gift, turned_end, gift_send, gift_recv, far_sums,
):
    me = lax.axis_index("tile")
    core = lax.axis_index("src")
    side = lax.rem(me, 2)
    level = me // 2
    levels = count_tile // 2
    step = 1 - 2 * side
    rows, half = win.shape[2], win.shape[3]
    tiles, kmax = table.shape
    out_rows = out_ref.shape[0]
    chunks, wide = w.shape[0], w.shape[3] // 2

    def inside(place):
        return (place >= 0) & (place < levels)

    has_near = inside(level + step)
    has_back = inside(level - step)
    has_far = inside(level - 2 * step)
    across = {"tile": me + step}
    forward = {"tile": me + 2 * step}
    backward = {"tile": me - 2 * step}
    partner = {"src": 1 - core}
    targets = (across, forward, backward, backward, across, forward)
    sends = (None, has_near, has_back, has_back, has_near, has_near & has_back)
    arrives = (None, has_back, has_near, has_near, has_back, has_far)

    ends = short_line(out_rows, levels) and levels == 4
    given = chunks - gift.shape[0] if ends else chunks
    gives = (level == 0) | (level == levels - 1)
    takes = (level == 1) | (level == levels - 2)
    giver = jnp.where(level == 1, 0, levels - 1)
    end_near = giver == level + step
    end_slot = jnp.where(end_near, NEAR, BACK)
    end_across = jnp.where(end_near, NEAR_ACROSS, BACK_ACROSS)

    def guarded(condition, run):
        if condition is None:
            run()
        else:
            pl.when(condition)(run)

    def remote(source, target, send, recv, device):
        return pltpu.make_async_remote_copy(
            src_ref=source, dst_ref=target, send_sem=send, recv_sem=recv,
            device_id=device, device_id_type=pl.DeviceIdType.MESH,
        )

    depth = rows // PIECES
    parts = 2 if rows % 256 == 0 else 1

    def piece(slot, index, count=1):
        return win.at[slot, :, pl.ds(index * depth, count * depth)]

    def route(number, index, count=1):
        source, target = ROUTES[number]
        if number in RELAYED:
            recv = relay_recv.at[RELAYED.index(number), index]
        else:
            recv = final_recv.at[number, index * parts // PIECES if number == 5 else 0]
        return remote(
            piece(source, index, count), piece(target, index, count), route_send.at[number], recv, targets[number]
        )

    def send_route(number, index):
        guarded(sends[number], lambda: route(number, index).start())

    def arrive(number, index, count=1):
        guarded(arrives[number], lambda: route(number, index, count).wait_recv())

    def to_pair(source, target, number):
        return remote(win.at[source], win.at[target], pair_send.at[number], pair_recv.at[number], partner)

    load_a = pltpu.make_async_copy(a_ref, win.at[OWN], load_sem.at[0])
    load_theirs = pltpu.make_async_copy(
        v_ref.at[:, :, pl.ds(pl.multiple_of((1 - core) * half, half), half)], vbuf.at[0], load_sem.at[1]
    )
    load_mine = pltpu.make_async_copy(
        v_ref.at[:, :, pl.ds(pl.multiple_of(core * half, half), half)], vbuf.at[1], load_sem.at[2]
    )
    load_table = pltpu.make_async_copy(partners_ref, table, load_sem.at[3])
    load_counts = pltpu.make_async_copy(counts_ref, sampled, load_sem.at[4])
    load_a.start()
    load_table.start()
    load_counts.start()
    load_theirs.start()
    load_mine.start()

    barrier = pltpu.get_barrier_semaphore()
    pl.semaphore_signal(barrier, inc=1, device_id=partner, device_id_type=pl.DeviceIdType.MESH)
    pl.semaphore_signal(barrier, inc=1, device_id=across, device_id_type=pl.DeviceIdType.MESH)

    def other_level(number):
        return lax.rem(level + 1 + number, levels)

    if short_line(out_rows, levels):
        for there, device in ((has_near, forward), (has_back, backward)):
            @pl.when(there)
            def _(device=device):
                pl.semaphore_signal(barrier, inc=1, device_id=device, device_id_type=pl.DeviceIdType.MESH)

        pl.semaphore_wait(barrier, 2 + has_near.astype(jnp.int32) + has_back.astype(jnp.int32))
    else:
        @pl.loop(0, levels - 1)
        def _(number):
            pl.semaphore_signal(
                barrier, inc=1, device_id={"tile": other_level(number) * 2 + side},
                device_id_type=pl.DeviceIdType.MESH,
            )

        pl.semaphore_wait(barrier, levels + 1)
    load_a.wait()
    for index in range(PIECES):
        for number in (0, 1, 2):
            send_route(number, index)
    to_pair(OWN, PAIR, 0).start()

    own = win[OWN].reshape(2 * rows, half)

    def images(slot):
        first = dot(own, vbuf[slot, 0], ((1,), (0,)))
        second = dot(own, vbuf[slot, 1], ((1,), (0,)))
        return first[:rows] - second[rows:], second[:rows] + first[rows:]

    load_theirs.wait()
    real, imag = images(0)
    ipart[0] = real
    ipart[1] = imag
    image_copy = remote(ipart, irecv, img_sem.at[0], img_sem.at[1], partner)
    image_copy.start()
    load_mine.wait()
    real, imag = images(1)
    image_copy.wait_recv()
    img[:rows] = (real + irecv[0]).astype(BF16)
    img[rows:] = (imag + irecv[1]).astype(BF16)

    load_table.wait()
    load_counts.wait()
    acc[...] = jnp.zeros_like(acc)

    def exists(slot):
        return (
            (slot <= ACROSS)
            | (((slot == NEAR) | (slot == NEAR_ACROSS)) & has_near)
            | (((slot == BACK) | (slot == BACK_ACROSS)) & has_back)
            | ((slot == FAR) & has_far)
        )

    def sample(slot):
        offset = 0
        for index, value in enumerate(OFFSETS):
            offset = jnp.where(slot == index, value, offset)
        first = (me + offset * step) * tiles
        tile = rows // tiles
        bands = []
        for row in range(tiles):
            blocks = []
            for column in range(tiles):
                hit = False
                for k in range(kmax):
                    hit = hit | ((table[row, k] == first + column) & (k < sampled[row]))
                blocks.append(jnp.full((tile, tile), jnp.where(hit, 1.0, 0.0), F32))
            bands.append(jnp.concatenate(blocks, axis=1))
        return jnp.concatenate(bands, axis=0)

    def couple_copy(slot):
        return remote(cpart.at[slot], crecv.at[slot], couple_send.at[slot], couple_recv.at[slot], partner)

    def couple(low, high):
        @pl.loop(low, high)
        def _(slot):
            @pl.when(exists(slot))
            def _():
                block = win[slot].reshape(2 * rows, half)
                prod = dot(img[...], block, ((1,), (1,)))
                cpart[slot, 0] = prod[:rows, :rows] + prod[rows:, rows:]
                cpart[slot, 1] = prod[rows:, :rows] - prod[:rows, rows:]
                couple_copy(slot).start()

    def weigh(low, high):
        @pl.loop(low, high)
        def _(slot):
            @pl.when(exists(slot))
            def _():
                couple_copy(slot).wait_recv()
                live = sample(slot)
                real = ((cpart[slot, 0] + crecv[slot, 0]) * live).astype(BF16)
                imag = ((cpart[slot, 1] + crecv[slot, 1]) * live).astype(BF16)
                left = jnp.concatenate(
                    [jnp.concatenate([real, -imag], axis=1), jnp.concatenate([imag, real], axis=1)], axis=0
                )
                acc[...] += dot(left, win[slot].reshape(2 * rows, half), ((1,), (0,)))

    def pass_on(index):
        arrive(0, index)
        send_route(3, index)
        arrive(2, index)
        send_route(4, index)

    couple(OWN, ACROSS)
    for index in range(PIECES):
        pass_on(index)
    to_pair(ACROSS, PAIR_ACROSS, 1).start()
    arrive(1, 0, PIECES)
    if ends:
        pl.when(takes)(lambda: to_pair(end_slot, PAIR_END, 2).start())
    span = max(out_rows, 128)

    def lay(target, group, block, slot, lanes):
        for part in range(2):
            first = (2 * part + block) * rows
            target[group, :, first : first + rows] = win[slot, part, :, lanes].T

    def turn_over():
        to_pair(OWN, PAIR, 0).wait_recv()
        to_pair(ACROSS, PAIR_ACROSS, 1).wait_recv()

        @pl.loop(0, turned.shape[0])
        def _(group):
            column = (2 * group + side) * out_rows if span == out_rows else group * span
            which = column // half
            base = jnp.where(which == core, OWN, PAIR)
            lanes = pl.ds(pl.multiple_of(column - which * half, 128), span)
            for block in range(2):
                lay(turned, group, block, base + block, lanes)

    jobs = (
        lambda: couple(ACROSS, BACK_ACROSS),
        lambda: weigh(OWN, NEAR),
        lambda: weigh(NEAR, BACK_ACROSS),
        turn_over,
    )
    for index in range(PIECES):
        for job in jobs[index * len(jobs) // PIECES : (index + 1) * len(jobs) // PIECES]:
            job()
        arrive(4, index)
        send_route(5, index)
    couple(BACK_ACROSS, NEAR_ACROSS)
    arrive(3, 0, PIECES)
    couple(NEAR_ACROSS, FAR)
    part_rows = rows // parts

    def far_part(part):
        return win[FAR, :, part * part_rows : (part + 1) * part_rows].reshape(2 * part_rows, half)

    def far_copy(part):
        return remote(
            far_sums.at[0, part], far_sums.at[1, part],
            couple_send.at[FAR + part], couple_recv.at[FAR + part], partner,
        )

    def couple_far(part):
        @pl.when(has_far)
        def _():
            arrive_far(part)
            prod = dot(img[...], far_part(part), ((1,), (1,)))
            for index, value in enumerate((
                prod[:rows, :part_rows] + prod[rows:, part_rows:],
                prod[rows:, :part_rows] - prod[:rows, part_rows:],
            )):
                far_sums[0, part, index] = value
            far_copy(part).start()

    def arrive_far(part):
        route(5, part * PIECES // parts, PIECES // parts).wait_recv()

    def weigh_far(part):
        @pl.when(has_far)
        def _():
            far_copy(part).wait_recv()
            columns = slice(part * part_rows, (part + 1) * part_rows)
            live = sample(FAR)[:, columns]
            real = ((far_sums[0, part, 0] + far_sums[1, part, 0]) * live).astype(BF16)
            imag = ((far_sums[0, part, 1] + far_sums[1, part, 1]) * live).astype(BF16)
            left = jnp.concatenate(
                [jnp.concatenate([real, -imag], axis=1), jnp.concatenate([imag, real], axis=1)], axis=0
            )
            acc[...] += dot(left, far_part(part), ((1,), (0,)))

    couple_far(0)
    weigh(BACK_ACROSS, FAR)
    for part in range(1, parts):
        couple_far(part)
        weigh_far(part - 1)
    weigh_far(parts - 1)

    def w_copy(chunk):
        return remote(w.at[chunk, 0], w.at[chunk, 1], w_send.at[0], w_recv.at[chunk], across)

    def halves(first, second):
        low = lax.broadcasted_iota(jnp.int32, first.shape, 1) < wide
        return (
            jnp.where(low, first, pltpu.roll(second, wide, 1)),
            jnp.where(low, pltpu.roll(first, wide, 1), second),
        )

    def gift_copy(index, hop):
        source = w.at[given + index, 0] if hop == 0 else gift.at[index, 0]
        device = {"tile": me + jnp.where(level == 0, 2, -2)} if hop == 0 else across
        return remote(
            source, gift.at[index, hop], gift_send.at[index, hop], gift_recv.at[index, hop], device
        )

    span_chunks = 2 if wide % 128 else 1
    for first in range(0, chunks, span_chunks):
        columns = slice(first * wide, (first + span_chunks) * wide)
        real, imag = acc[:rows, columns], acc[rows:, columns]
        if wide % 128:
            packed = halves(real, imag)
        else:
            packed = (jnp.concatenate([real, imag], axis=1),)
        for index, value in enumerate(packed):
            w[first + index, 0] = value.astype(BF16)
            w_copy(first + index).start()

    def give(when):
        @pl.when(gives & when)
        def _():
            for index in range(chunks - given):
                gift_copy(index, 0).start()

    if ends:
        give(jnp.logical_not(has_far))

        pl.when(takes)(lambda: to_pair(end_across, PAIR_END_ACROSS, 3).start())

    def turn_end():
        @pl.when(takes)
        def _():
            to_pair(end_slot, PAIR_END, 2).wait_recv()
            to_pair(end_across, PAIR_END_ACROSS, 3).wait_recv()
            for group in range(levels):
                column = (2 * group + side) * out_rows
                which = column // half
                lanes = pl.ds(pl.multiple_of(column - which * half, 128), span)
                for block, (here, there) in enumerate(((end_slot, PAIR_END), (end_across, PAIR_END_ACROSS))):
                    lay(turned_end, group, block, jnp.where(which == core, here, there), lanes)

    def product(left, right):
        straight = dot(left[:, : 2 * rows], right, ((1,), (0,)))
        crossed = pltpu.roll(dot(left[:, 2 * rows :], right, ((1,), (0,))), wide, 1)
        low = lax.broadcasted_iota(jnp.int32, crossed.shape, 1) < wide
        return straight + jnp.where(low, crossed, -crossed)

    def partial(chunk, group):
        return product(turned[group], w[chunk].reshape(2 * rows, 2 * wide))

    def rows_of(target):
        return pl.multiple_of((2 * target + side) * out_rows, out_rows)

    def put(chunk, total):
        for part in range(2):
            for index in range(wide // 128):
                first = part * wide + index * 128
                out_ref[:, 2 * (chunk * wide // 128 + index) + part] = total[:, first : first + 128]

    def term(chunk, lane, slot, target, level_to, arrival=None):
        return remote(
            hp.at[chunk, pl.ds(rows_of(target), out_rows)], hr.at[chunk, lane, slot],
            h_send.at[0], h_recv.at[chunk, slot if arrival is None else arrival], {"tile": 2 * level_to + side},
        )

    def settle():
        for number in range(len(ROUTES)):
            guarded(sends[number], lambda number=number: route(number, 0, PIECES).wait_send())
        to_pair(OWN, PAIR, 0).wait_send()
        to_pair(ACROSS, PAIR_ACROSS, 1).wait_send()
        image_copy.wait_send()

        @pl.loop(0, FAR)
        def _(slot):
            @pl.when(exists(slot))
            def _():
                couple_copy(slot).wait_send()

        @pl.when(has_far)
        def _():
            for part in range(parts):
                far_copy(part).wait_send()

        if ends:
            @pl.when(gives)
            def _():
                for index in range(chunks - given):
                    gift_copy(index, 0).wait_send()

            @pl.when(takes)
            def _():
                for index in range(chunks - given):
                    gift_copy(index, 1).wait_send()
                to_pair(end_slot, PAIR_END, 2).wait_send()
                to_pair(end_across, PAIR_END_ACROSS, 3).wait_send()

        remote(w.at[:, 0], w.at[:, 1], w_send.at[0], w_recv.at[0], across).wait_send()

        def sent(count):
            rows_sent = hp.at[:count, pl.ds(0, (levels - 1) * out_rows)]
            remote(rows_sent, rows_sent, h_send.at[0], h_recv.at[0, 0], across).wait_send()

        if levels > 1:
            if given == chunks:
                sent(chunks)
            else:
                pl.when(gives)(lambda: sent(given))
                pl.when(takes)(lambda: sent(chunks))

    if short_line(out_rows, levels):
        depths = level, levels - 1 - level

        def total(chunk):
            w_copy(chunk).wait_recv()
            every = turned[...].reshape(levels * out_rows, 4 * rows)
            tot[chunk] = product(every, w[chunk].reshape(2 * rows, 2 * wide)).reshape(levels, out_rows, 2 * wide)

        def place(target):
            return pl.ds(rows_of(target), out_rows)

        def far(lane, number):
            return levels - 1 - number if lane == 0 else number

        def passing(chunk, lane, target, number):
            arrival = number if number < levels - 2 else 2 + lane
            return term(chunk, lane, target, target, level + 1 - 2 * lane, arrival)

        def begin(chunk, numbers):
            for lane in range(2):
                for number in numbers:
                    target = far(lane, number)

                    @pl.when(depths[lane] == 0)
                    def _(lane=lane, target=target, number=number):
                        hp[chunk, place(target)] = tot[chunk, target].astype(BF16)
                        passing(chunk, lane, target, number).start()

        def beside(chunk):
            for lane in range(2):
                target = far(lane, 0)

                @pl.when(depths[lane] == 2)
                def _(lane=lane, target=target):
                    hp[chunk, place(target)] = tot[chunk, target].astype(BF16)
                    term(chunk, lane, levels, target, target, 0).start()

        def add_on(chunk, number):
            for lane in range(2):
                target = far(lane, number)

                @pl.when(depths[lane] == 1)
                def _(lane=lane, target=target):
                    value = tot[chunk, target]
                    if chunk < given:
                        passing(chunk, lane, target, number).wait_recv()
                        value = value + hr[chunk, lane, target].astype(F32)
                    hp[chunk, place(target)] = value.astype(BF16)
                    term(chunk, lane, target, target, target, 2 + lane).start()

        def pass_gift(index):
            @pl.when(takes)
            def _():
                gift_copy(index, 0).wait_recv()
                gift_copy(index, 1).start()

        def use_gift(index):
            @pl.when(takes)
            def _():
                gift_copy(index, 1).wait_recv()
                every = turned_end[...].reshape(levels * out_rows, 4 * rows)
                more = product(every, gift[index].reshape(2 * rows, 2 * wide)).reshape(levels, out_rows, 2 * wide)
                for target in range(1, levels - 1):
                    tot[given + index, target] += more[target]
                far_end = jnp.where(level == 1, levels - 1, 0)
                tot[given + index, far_end] += jnp.where(level == 1, more[levels - 1], more[0])

        distant = range(levels - 2)

        for chunk in range(chunks + 1):
            if chunk < chunks:
                total(chunk)
                if chunk < given:
                    begin(chunk, distant)
                if levels > 3:
                    beside(chunk)
            if ends and chunk == GIVE_AT:
                give(has_far)
            if chunk == given - 1 and levels > 1:
                for done in range(given):
                    begin(done, (levels - 2,))
            if ends and chunk == TURN_AT:
                turn_end()
            if 0 <= chunk - PASS_AT < chunks - given:
                pass_gift(chunk - PASS_AT)
            if chunk > given:
                use_gift(chunk - 1 - given)
            if chunk > 0:
                for number in distant:
                    add_on(chunk - 1, number)

        for chunk in range(chunks):
            if chunk == chunks - 1:
                settle()
            for lane, slot, arrival, there in (
                (0, level, 2, depths[0] > (1 if chunk >= given else 0)),
                (1, level, 3, depths[1] > (1 if chunk >= given else 0)),
                (0, levels, 0, depths[0] > 2), (1, levels, 0, depths[1] > 2),
            ):
                @pl.when(there)
                def _(chunk=chunk, lane=lane, slot=slot, arrival=arrival):
                    term(chunk, lane, slot, level, level, arrival).wait_recv()
                    tot[chunk, level] += hr[chunk, lane, slot].astype(F32)
            if wide % 128 == 0:
                put(chunk, tot[chunk, level])
            elif chunk % 2:
                for part, value in enumerate(halves(tot[chunk - 1, level], tot[chunk, level])):
                    out_ref[:, chunk - 1 + part] = value
    else:
        for chunk in range(chunks):
            w_copy(chunk).wait_recv()
            if span != out_rows:
                @pl.loop(0, hp.shape[1] // span)
                def _(group):
                    column = pl.multiple_of(group * span, span)
                    hp[chunk, pl.ds(column, span)] = partial(chunk, group).astype(BF16)

            @pl.loop(0, levels - 1)
            def _(number):
                target = other_level(number)
                if span == out_rows:
                    hp[chunk, pl.ds(rows_of(target), out_rows)] = partial(chunk, target).astype(BF16)
                term(chunk, 0, level, target, target).start()

            if span == out_rows:
                hp[chunk, pl.ds(rows_of(level), out_rows)] = partial(chunk, level).astype(BF16)

        for chunk in range(chunks):
            def add(number, total):
                sender = other_level(number)
                term(chunk, 0, sender, level, sender).wait_recv()
                return total + hr[chunk, 0, sender].astype(F32)

            put(chunk, lax.fori_loop(0, levels - 1, add, hp[chunk, pl.ds(rows_of(level), out_rows)].astype(F32)))

        settle()

def shards(count_tile, green, direction, partners, counts):
    tile_dev, kmax = partners.shape
    rows, half = green.shape[1:]
    sources = direction.shape[2]
    out_rows = sources // count_tile
    levels = count_tile // 2
    chunks = SHORT_CHUNKS if short_line(out_rows, levels) else CHUNKS
    wide = half // chunks
    parts = 2 if rows % 256 == 0 else 1
    lanes = 2 if short_line(out_rows, levels) else 1
    anywhere = pl.BlockSpec(memory_space=pl.ANY)
    local = pl.BlockSpec(memory_space=pltpu.VMEM)
    dma = pltpu.SemaphoreType.DMA
    out = pl.pallas_call(
        functools.partial(kernel, count_tile),
        out_shape=jax.ShapeDtypeStruct((out_rows, half // 64, 128), F32),
        in_specs=[anywhere] * 4,
        out_specs=local,
        scratch_shapes=[
            pltpu.SMEM((tile_dev, kmax), jnp.int32),
            pltpu.SMEM((tile_dev,), jnp.int32),
            pltpu.VMEM((PAIR_END_ACROSS + 1, 2, rows, half), BF16),
            pltpu.VMEM((2, 2, half, half), BF16),
            pltpu.VMEM((2 * rows, half), BF16),
            pltpu.VMEM((2, rows, half), F32),
            pltpu.VMEM((2, rows, half), F32),
            pltpu.VMEM((FAR, 2, rows, rows), F32),
            pltpu.VMEM((FAR, 2, rows, rows), F32),
            pltpu.VMEM((2 * rows, half), F32),
            pltpu.VMEM((chunks, 2, rows, 2 * wide), BF16),
            pltpu.VMEM((levels if out_rows >= 128 else sources // 128, max(out_rows, 128), 4 * rows), BF16),
            pltpu.VMEM((chunks, sources, 2 * wide), BF16),
            pltpu.VMEM((chunks, lanes, levels + 1, out_rows, 2 * wide), BF16),
            dma((5,)),
            dma((2,)),
            dma((len(ROUTES),)),
            dma((len(RELAYED), PIECES)),
            dma((len(ROUTES), 2)),
            dma((FAR + 2,)),
            dma((FAR + 2,)),
            dma((4,)),
            dma((4,)),
            dma((1,)),
            dma((chunks,)),
            dma((1,)),
            dma((chunks, 4 if lanes == 2 else levels + 1)),
            pltpu.VMEM((chunks, levels, out_rows, 2 * wide) if lanes == 2 else (1, 1, 8, 128), F32),
            pltpu.VMEM((GIFTS, 2, rows, 2 * wide), BF16),
            pltpu.VMEM((levels, out_rows, 4 * rows) if lanes == 2 else (1, 16, 128), BF16),
            dma((GIFTS, 2)),
            dma((GIFTS, 2)),
            pltpu.VMEM((2, parts, 2, rows, rows // parts), F32),
        ],
        compiler_params=pltpu.CompilerParams(
            collective_id=0, has_side_effects=True, vmem_limit_bytes=56 * 1024 * 1024
        ),
    )(green, direction, partners, counts)
    out = out.reshape(out_rows, half // 128, 2, 128)
    return jnp.swapaxes(out, 1, 2).reshape(out_rows, 2, half)


def solution(mesh):
    in_specs = (
        P(None, ("freq", "tile"), "src"),
        P(None, ("freq", "src"), None),
        P(("freq", "tile"), None),
        P(("freq", "tile")),
    )
    out_specs = P(("freq", "tile"), None, "src")
    body = functools.partial(shards, mesh.shape["tile"])
    return jax.shard_map(body, mesh=mesh, in_specs=in_specs, out_specs=out_specs, check_vma=False)
```

```python
import functools

import jax
import jax.numpy as jnp
from jax import lax
from jax.experimental import pallas as pl
from jax.experimental.pallas import tpu as pltpu
from jax.sharding import PartitionSpec as P

BAND_DEV = 3
PIECES = 8
CHUNKS = 4
SHORT_CHUNKS = 8
GIFTS = 1
PASS_AT = 2
TURN_AT = 4
GIVE_AT = 0
OWN, ACROSS, NEAR, BACK, BACK_ACROSS, NEAR_ACROSS, FAR, PAIR, PAIR_ACROSS, PAIR_END, PAIR_END_ACROSS = range(11)
OFFSETS = (0, 1, 2, -2, -1, 3, -3)
ROUTES = (
    (OWN, ACROSS),
    (OWN, BACK),
    (OWN, NEAR),
    (ACROSS, NEAR_ACROSS),
    (NEAR, BACK_ACROSS),
    (BACK_ACROSS, FAR),
)
RELAYED = (0, 2, 4)
FINAL = (1, 3, 5)
F32 = jnp.float32
BF16 = jnp.bfloat16


def dot(left, right, dims):
    return lax.dot_general(left, right, (dims, ((), ())), preferred_element_type=F32)


def short_line(out_rows, levels):
    return out_rows % 128 == 0 and levels <= 4


def kernel(
    count_tile, a_ref, v_ref, partners_ref, counts_ref, out_ref,
    table, sampled, win, vbuf, img, ipart, irecv, cpart, crecv, acc, w, turned, hp, hr,
    load_sem, img_sem, route_send, relay_recv, final_recv, couple_send, couple_recv,
    pair_send, pair_recv, w_send, w_recv, h_send, h_recv, tot,
    gift, turned_end, gift_send, gift_recv, far_sums,
):
    me = lax.axis_index("tile")
    core = lax.axis_index("src")
    side = lax.rem(me, 2)
    level = me // 2
    levels = count_tile // 2
    step = 1 - 2 * side
    rows, half = win.shape[2], win.shape[3]
    tiles, kmax = table.shape
    out_rows = out_ref.shape[0]
    chunks, wide = w.shape[0], w.shape[3] // 2

    def inside(place):
        return (place >= 0) & (place < levels)

    has_near = inside(level + step)
    has_back = inside(level - step)
    has_far = inside(level - 2 * step)
    across = {"tile": me + step}
    forward = {"tile": me + 2 * step}
    backward = {"tile": me - 2 * step}
    partner = {"src": 1 - core}
    targets = (across, forward, backward, backward, across, forward)
    sends = (None, has_near, has_back, has_back, has_near, has_near & has_back)
    arrives = (None, has_back, has_near, has_near, has_back, has_far)

    ends = short_line(out_rows, levels) and levels == 4
    given = chunks - gift.shape[0] if ends else chunks
    gives = (level == 0) | (level == levels - 1)
    takes = (level == 1) | (level == levels - 2)
    giver = jnp.where(level == 1, 0, levels - 1)
    end_near = giver == level + step
    end_slot = jnp.where(end_near, NEAR, BACK)
    end_across = jnp.where(end_near, NEAR_ACROSS, BACK_ACROSS)

    def guarded(condition, run):
        if condition is None:
            run()
        else:
            pl.when(condition)(run)

    def remote(source, target, send, recv, device):
        return pltpu.make_async_remote_copy(
            src_ref=source, dst_ref=target, send_sem=send, recv_sem=recv,
            device_id=device, device_id_type=pl.DeviceIdType.MESH,
        )

    depth = rows // PIECES
    parts = 2 if rows % 256 == 0 else 1

    def piece(slot, index, count=1):
        return win.at[slot, :, pl.ds(index * depth, count * depth)]

    def route(number, index, count=1):
        source, target = ROUTES[number]
        if number in RELAYED:
            recv = relay_recv.at[RELAYED.index(number), index]
        else:
            recv = final_recv.at[FINAL.index(number) + (index * parts // PIECES if number == 5 else 0)]
        return remote(
            piece(source, index, count), piece(target, index, count), route_send.at[number], recv, targets[number]
        )

    def send_route(number, index):
        guarded(sends[number], lambda: route(number, index).start())

    def arrive(number, index, count=1):
        guarded(arrives[number], lambda: route(number, index, count).wait_recv())

    def to_pair(source, target, number):
        return remote(win.at[source], win.at[target], pair_send.at[number], pair_recv.at[number], partner)

    load_a = pltpu.make_async_copy(a_ref, win.at[OWN], load_sem.at[0])
    load_theirs = pltpu.make_async_copy(
        v_ref.at[:, :, pl.ds(pl.multiple_of((1 - core) * half, half), half)], vbuf.at[0], load_sem.at[1]
    )
    load_mine = pltpu.make_async_copy(
        v_ref.at[:, :, pl.ds(pl.multiple_of(core * half, half), half)], vbuf.at[1], load_sem.at[2]
    )
    load_table = pltpu.make_async_copy(partners_ref, table, load_sem.at[3])
    load_counts = pltpu.make_async_copy(counts_ref, sampled, load_sem.at[4])
    load_a.start()
    load_table.start()
    load_counts.start()
    load_theirs.start()
    load_mine.start()

    barrier = pltpu.get_barrier_semaphore()
    pl.semaphore_signal(barrier, inc=1, device_id=partner, device_id_type=pl.DeviceIdType.MESH)
    pl.semaphore_signal(barrier, inc=1, device_id=across, device_id_type=pl.DeviceIdType.MESH)

    def other_level(number):
        return lax.rem(level + 1 + number, levels)

    if short_line(out_rows, levels):
        for there, device in ((has_near, forward), (has_back, backward)):
            @pl.when(there)
            def _(device=device):
                pl.semaphore_signal(barrier, inc=1, device_id=device, device_id_type=pl.DeviceIdType.MESH)

        pl.semaphore_wait(barrier, 2 + has_near.astype(jnp.int32) + has_back.astype(jnp.int32))
    else:
        @pl.loop(0, levels - 1)
        def _(number):
            pl.semaphore_signal(
                barrier, inc=1, device_id={"tile": other_level(number) * 2 + side},
                device_id_type=pl.DeviceIdType.MESH,
            )

        pl.semaphore_wait(barrier, levels + 1)
    load_a.wait()
    for index in range(PIECES):
        for number in (0, 1, 2):
            send_route(number, index)
    to_pair(OWN, PAIR, 0).start()

    own = win[OWN].reshape(2 * rows, half)

    def images(slot):
        first = dot(own, vbuf[slot, 0], ((1,), (0,)))
        second = dot(own, vbuf[slot, 1], ((1,), (0,)))
        return first[:rows] - second[rows:], second[:rows] + first[rows:]

    load_theirs.wait()
    real, imag = images(0)
    ipart[0] = real
    ipart[1] = imag
    image_copy = remote(ipart, irecv, img_sem.at[0], img_sem.at[1], partner)
    image_copy.start()
    load_mine.wait()
    real, imag = images(1)
    image_copy.wait_recv()
    img[:rows] = (real + irecv[0]).astype(BF16)
    img[rows:] = (imag + irecv[1]).astype(BF16)

    load_table.wait()
    load_counts.wait()
    acc[...] = jnp.zeros_like(acc)

    def exists(slot):
        return (
            (slot <= ACROSS)
            | (((slot == NEAR) | (slot == NEAR_ACROSS)) & has_near)
            | (((slot == BACK) | (slot == BACK_ACROSS)) & has_back)
            | ((slot == FAR) & has_far)
        )

    def sample(slot):
        offset = 0
        for index, value in enumerate(OFFSETS):
            offset = jnp.where(slot == index, value, offset)
        first = (me + offset * step) * tiles
        tile = rows // tiles
        bands = []
        for row in range(tiles):
            blocks = []
            for column in range(tiles):
                hit = False
                for k in range(kmax):
                    hit = hit | ((table[row, k] == first + column) & (k < sampled[row]))
                blocks.append(jnp.full((tile, tile), jnp.where(hit, 1.0, 0.0), F32))
            bands.append(jnp.concatenate(blocks, axis=1))
        return jnp.concatenate(bands, axis=0)

    def couple_copy(slot):
        return remote(cpart.at[slot], crecv.at[slot], couple_send.at[slot], couple_recv.at[slot], partner)

    def couple(low, high):
        @pl.loop(low, high)
        def _(slot):
            @pl.when(exists(slot))
            def _():
                block = win[slot].reshape(2 * rows, half)
                prod = dot(img[...], block, ((1,), (1,)))
                cpart[slot, 0] = prod[:rows, :rows] + prod[rows:, rows:]
                cpart[slot, 1] = prod[rows:, :rows] - prod[:rows, rows:]
                couple_copy(slot).start()

    def weigh(low, high):
        @pl.loop(low, high)
        def _(slot):
            @pl.when(exists(slot))
            def _():
                couple_copy(slot).wait_recv()
                live = sample(slot)
                real = ((cpart[slot, 0] + crecv[slot, 0]) * live).astype(BF16)
                imag = ((cpart[slot, 1] + crecv[slot, 1]) * live).astype(BF16)
                left = jnp.concatenate(
                    [jnp.concatenate([real, -imag], axis=1), jnp.concatenate([imag, real], axis=1)], axis=0
                )
                acc[...] += dot(left, win[slot].reshape(2 * rows, half), ((1,), (0,)))

    def pass_on(index):
        arrive(0, index)
        send_route(3, index)
        arrive(2, index)
        send_route(4, index)

    couple(OWN, ACROSS)
    for index in range(PIECES):
        pass_on(index)
    to_pair(ACROSS, PAIR_ACROSS, 1).start()
    arrive(1, 0, PIECES)
    if ends:
        pl.when(takes)(lambda: to_pair(end_slot, PAIR_END, 2).start())
    span = max(out_rows, 128)

    def lay(target, group, block, slot, lanes):
        for part in range(2):
            first = (2 * block + part) * rows
            target[group, :, first : first + rows] = win[slot, part, :, lanes].T

    def turn_over():
        to_pair(OWN, PAIR, 0).wait_recv()
        to_pair(ACROSS, PAIR_ACROSS, 1).wait_recv()

        @pl.loop(0, turned.shape[0])
        def _(group):
            column = (2 * group + side) * out_rows if span == out_rows else group * span
            which = column // half
            base = jnp.where(which == core, OWN, PAIR)
            lanes = pl.ds(pl.multiple_of(column - which * half, 128), span)
            for block in range(2):
                lay(turned, group, block, base + block, lanes)

    jobs = (
        lambda: couple(ACROSS, BACK_ACROSS),
        lambda: weigh(OWN, NEAR),
        lambda: weigh(NEAR, BACK_ACROSS),
        turn_over,
    )
    for index in range(PIECES):
        for job in jobs[index * len(jobs) // PIECES : (index + 1) * len(jobs) // PIECES]:
            job()
        arrive(4, index)
        send_route(5, index)
    couple(BACK_ACROSS, NEAR_ACROSS)
    arrive(3, 0, PIECES)
    couple(NEAR_ACROSS, FAR)
    part_rows = rows // parts

    def far_part(part):
        return win[FAR, :, part * part_rows : (part + 1) * part_rows].reshape(2 * part_rows, half)

    def far_copy(part):
        return remote(
            far_sums.at[0, part], far_sums.at[1, part],
            couple_send.at[FAR + part], couple_recv.at[FAR + part], partner,
        )

    def couple_far(part):
        @pl.when(has_far)
        def _():
            arrive_far(part)
            prod = dot(img[...], far_part(part), ((1,), (1,)))
            for index, value in enumerate((
                prod[:rows, :part_rows] + prod[rows:, part_rows:],
                prod[rows:, :part_rows] - prod[:rows, part_rows:],
            )):
                far_sums[0, part, index] = value
            far_copy(part).start()

    def arrive_far(part):
        route(5, part * PIECES // parts, PIECES // parts).wait_recv()

    def weigh_far(part):
        @pl.when(has_far)
        def _():
            far_copy(part).wait_recv()
            columns = slice(part * part_rows, (part + 1) * part_rows)
            live = sample(FAR)[:, columns]
            real = ((far_sums[0, part, 0] + far_sums[1, part, 0]) * live).astype(BF16)
            imag = ((far_sums[0, part, 1] + far_sums[1, part, 1]) * live).astype(BF16)
            left = jnp.concatenate(
                [jnp.concatenate([real, -imag], axis=1), jnp.concatenate([imag, real], axis=1)], axis=0
            )
            acc[...] += dot(left, far_part(part), ((1,), (0,)))

    couple_far(0)
    weigh(BACK_ACROSS, FAR)
    for part in range(1, parts):
        couple_far(part)
        weigh_far(part - 1)
    weigh_far(parts - 1)

    def w_copy(chunk):
        return remote(w.at[chunk, 0], w.at[chunk, 1], w_send.at[0], w_recv.at[chunk], across)

    def halves(first, second):
        low = lax.broadcasted_iota(jnp.int32, first.shape, 1) < wide
        return (
            jnp.where(low, first, pltpu.roll(second, wide, 1)),
            jnp.where(low, pltpu.roll(first, wide, 1), second),
        )

    def gift_copy(index, hop):
        source = w.at[given + index, 0] if hop == 0 else gift.at[index, 0]
        device = {"tile": me + jnp.where(level == 0, 2, -2)} if hop == 0 else across
        return remote(
            source, gift.at[index, hop], gift_send.at[index, hop], gift_recv.at[index, hop], device
        )

    span_chunks = 2 if wide % 128 else 1
    for first in range(0, chunks, span_chunks):
        columns = slice(first * wide, (first + span_chunks) * wide)
        real, imag = acc[:rows, columns], acc[rows:, columns]
        if wide % 128:
            packed = halves(real, imag)
        else:
            packed = (jnp.concatenate([real, imag], axis=1),)
        for index, value in enumerate(packed):
            w[first + index, 0] = value.astype(BF16)
            w_copy(first + index).start()

    def give(when):
        @pl.when(gives & when)
        def _():
            for index in range(chunks - given):
                gift_copy(index, 0).start()

    if ends:
        give(jnp.logical_not(has_far))

        pl.when(takes)(lambda: to_pair(end_across, PAIR_END_ACROSS, 3).start())

    def turn_end():
        @pl.when(takes)
        def _():
            to_pair(end_slot, PAIR_END, 2).wait_recv()
            to_pair(end_across, PAIR_END_ACROSS, 3).wait_recv()
            for group in range(levels):
                column = (2 * group + side) * out_rows
                which = column // half
                lanes = pl.ds(pl.multiple_of(column - which * half, 128), span)
                for block, (here, there) in enumerate(((end_slot, PAIR_END), (end_across, PAIR_END_ACROSS))):
                    lay(turned_end, group, block, jnp.where(which == core, here, there), lanes)

    def product(left, right):
        depth = left.shape[1] // 2
        straight = dot(left[:, :depth], right, ((1,), (0,)))
        crossed = pltpu.roll(dot(left[:, depth:], right, ((1,), (0,))), wide, 1)
        low = lax.broadcasted_iota(jnp.int32, crossed.shape, 1) < wide
        return straight + jnp.where(low, crossed, -crossed)

    def block_product(left, block, right):
        every = left[:, :, block * 2 * rows : (block + 1) * 2 * rows].reshape(levels * out_rows, 2 * rows)
        return product(every, right).reshape(levels, out_rows, 2 * wide)

    def partial(chunk, group):
        left = turned[group]
        return product(left[:, : 2 * rows], w[chunk, 0]) + product(left[:, 2 * rows :], w[chunk, 1])

    def rows_of(target):
        return pl.multiple_of((2 * target + side) * out_rows, out_rows)

    def put(chunk, total):
        for part in range(2):
            for index in range(wide // 128):
                first = part * wide + index * 128
                out_ref[:, 2 * (chunk * wide // 128 + index) + part] = total[:, first : first + 128]

    def term(chunk, lane, slot, target, level_to, arrival=None):
        return remote(
            hp.at[chunk, pl.ds(rows_of(target), out_rows)], hr.at[chunk, lane, slot],
            h_send.at[0], h_recv.at[chunk, slot if arrival is None else arrival], {"tile": 2 * level_to + side},
        )

    def settle():
        for number in range(len(ROUTES)):
            guarded(sends[number], lambda number=number: route(number, 0, PIECES).wait_send())
        to_pair(OWN, PAIR, 0).wait_send()
        to_pair(ACROSS, PAIR_ACROSS, 1).wait_send()
        image_copy.wait_send()

        @pl.loop(0, FAR)
        def _(slot):
            @pl.when(exists(slot))
            def _():
                couple_copy(slot).wait_send()

        @pl.when(has_far)
        def _():
            for part in range(parts):
                far_copy(part).wait_send()

        if ends:
            @pl.when(gives)
            def _():
                for index in range(chunks - given):
                    gift_copy(index, 0).wait_send()

            @pl.when(takes)
            def _():
                for index in range(chunks - given):
                    gift_copy(index, 1).wait_send()
                to_pair(end_slot, PAIR_END, 2).wait_send()
                to_pair(end_across, PAIR_END_ACROSS, 3).wait_send()

        remote(w.at[:, 0], w.at[:, 1], w_send.at[0], w_recv.at[0], across).wait_send()

        def sent(count):
            rows_sent = hp.at[:count, pl.ds(0, (levels - 1) * out_rows)]
            remote(rows_sent, rows_sent, h_send.at[0], h_recv.at[0, 0], across).wait_send()

        if levels > 1:
            if given == chunks:
                sent(chunks)
            else:
                pl.when(gives)(lambda: sent(given))
                pl.when(takes)(lambda: sent(chunks))

    if short_line(out_rows, levels):
        depths = level, levels - 1 - level

        def total(chunk):
            tot[chunk] = block_product(turned, 0, w[chunk, 0])
            w_copy(chunk).wait_recv()
            tot[chunk] += block_product(turned, 1, w[chunk, 1])

        def place(target):
            return pl.ds(rows_of(target), out_rows)

        def far(lane, number):
            return levels - 1 - number if lane == 0 else number

        def passing(chunk, lane, target, number):
            arrival = number if number < levels - 2 else 2 + lane
            return term(chunk, lane, target, target, level + 1 - 2 * lane, arrival)

        def begin(chunk, numbers):
            for lane in range(2):
                for number in numbers:
                    target = far(lane, number)

                    @pl.when(depths[lane] == 0)
                    def _(lane=lane, target=target, number=number):
                        hp[chunk, place(target)] = tot[chunk, target].astype(BF16)
                        passing(chunk, lane, target, number).start()

        def beside(chunk):
            for lane in range(2):
                target = far(lane, 0)

                @pl.when(depths[lane] == 2)
                def _(lane=lane, target=target):
                    hp[chunk, place(target)] = tot[chunk, target].astype(BF16)
                    term(chunk, lane, levels, target, target, 0).start()

        def add_on(chunk, number):
            for lane in range(2):
                target = far(lane, number)

                @pl.when(depths[lane] == 1)
                def _(lane=lane, target=target):
                    value = tot[chunk, target]
                    if chunk < given:
                        passing(chunk, lane, target, number).wait_recv()
                        value = value + hr[chunk, lane, target].astype(F32)
                    hp[chunk, place(target)] = value.astype(BF16)
                    term(chunk, lane, target, target, target, 2 + lane).start()

        def pass_gift(index):
            @pl.when(takes)
            def _():
                gift_copy(index, 0).wait_recv()
                gift_copy(index, 1).start()

        def use_gift(index, block):
            @pl.when(takes)
            def _():
                if block:
                    gift_copy(index, 1).wait_recv()
                more = block_product(turned_end, block, gift[index, block])
                for target in range(1, levels - 1):
                    tot[given + index, target] += more[target]
                far_end = jnp.where(level == 1, levels - 1, 0)
                tot[given + index, far_end] += jnp.where(level == 1, more[levels - 1], more[0])

        distant = range(levels - 2)

        for chunk in range(chunks + 1):
            if chunk < chunks:
                total(chunk)
                if chunk < given:
                    begin(chunk, distant)
                if levels > 3:
                    beside(chunk)
            if ends and chunk == GIVE_AT:
                give(has_far)
            if chunk == given - 1 and levels > 1:
                for done in range(given):
                    begin(done, (levels - 2,))
            if ends and chunk == TURN_AT:
                turn_end()
            if 0 <= chunk - PASS_AT < chunks - given:
                pass_gift(chunk - PASS_AT)
            if ends and chunk == given:
                use_gift(0, 0)
                add_on(chunk - 1, 0)
                use_gift(0, 1)
                for number, done in ((0, chunk), (1, chunk - 1), (1, chunk)):
                    add_on(done, number)
            elif 0 < chunk < given or given == chunks == chunk:
                for number in distant:
                    add_on(chunk - 1, number)

        for chunk in range(chunks):
            if chunk == chunks - 1:
                settle()
            for lane, slot, arrival, there in (
                (0, level, 2, depths[0] > (1 if chunk >= given else 0)),
                (1, level, 3, depths[1] > (1 if chunk >= given else 0)),
                (0, levels, 0, depths[0] > 2), (1, levels, 0, depths[1] > 2),
            ):
                @pl.when(there)
                def _(chunk=chunk, lane=lane, slot=slot, arrival=arrival):
                    term(chunk, lane, slot, level, level, arrival).wait_recv()
                    tot[chunk, level] += hr[chunk, lane, slot].astype(F32)
            if wide % 128 == 0:
                put(chunk, tot[chunk, level])
            elif chunk % 2:
                for part, value in enumerate(halves(tot[chunk - 1, level], tot[chunk, level])):
                    out_ref[:, chunk - 1 + part] = value
    else:
        for chunk in range(chunks):
            w_copy(chunk).wait_recv()
            if span != out_rows:
                @pl.loop(0, hp.shape[1] // span)
                def _(group):
                    column = pl.multiple_of(group * span, span)
                    hp[chunk, pl.ds(column, span)] = partial(chunk, group).astype(BF16)

            @pl.loop(0, levels - 1)
            def _(number):
                target = other_level(number)
                if span == out_rows:
                    hp[chunk, pl.ds(rows_of(target), out_rows)] = partial(chunk, target).astype(BF16)
                term(chunk, 0, level, target, target).start()

            if span == out_rows:
                hp[chunk, pl.ds(rows_of(level), out_rows)] = partial(chunk, level).astype(BF16)

        for chunk in range(chunks):
            def add(number, total):
                sender = other_level(number)
                term(chunk, 0, sender, level, sender).wait_recv()
                return total + hr[chunk, 0, sender].astype(F32)

            put(chunk, lax.fori_loop(0, levels - 1, add, hp[chunk, pl.ds(rows_of(level), out_rows)].astype(F32)))

        settle()

def shards(count_tile, green, direction, partners, counts):
    tile_dev, kmax = partners.shape
    rows, half = green.shape[1:]
    sources = direction.shape[2]
    out_rows = sources // count_tile
    levels = count_tile // 2
    chunks = SHORT_CHUNKS if short_line(out_rows, levels) else CHUNKS
    wide = half // chunks
    parts = 2 if rows % 256 == 0 else 1
    lanes = 2 if short_line(out_rows, levels) else 1
    anywhere = pl.BlockSpec(memory_space=pl.ANY)
    local = pl.BlockSpec(memory_space=pltpu.VMEM)
    dma = pltpu.SemaphoreType.DMA
    out = pl.pallas_call(
        functools.partial(kernel, count_tile),
        out_shape=jax.ShapeDtypeStruct((out_rows, half // 64, 128), F32),
        in_specs=[anywhere] * 4,
        out_specs=local,
        scratch_shapes=[
            pltpu.SMEM((tile_dev, kmax), jnp.int32),
            pltpu.SMEM((tile_dev,), jnp.int32),
            pltpu.VMEM((PAIR_END_ACROSS + 1, 2, rows, half), BF16),
            pltpu.VMEM((2, 2, half, half), BF16),
            pltpu.VMEM((2 * rows, half), BF16),
            pltpu.VMEM((2, rows, half), F32),
            pltpu.VMEM((2, rows, half), F32),
            pltpu.VMEM((FAR, 2, rows, rows), F32),
            pltpu.VMEM((FAR, 2, rows, rows), F32),
            pltpu.VMEM((2 * rows, half), F32),
            pltpu.VMEM((chunks, 2, rows, 2 * wide), BF16),
            pltpu.VMEM((levels if out_rows >= 128 else sources // 128, max(out_rows, 128), 4 * rows), BF16),
            pltpu.VMEM((chunks, sources, 2 * wide), BF16),
            pltpu.VMEM((chunks, lanes, levels + 1, out_rows, 2 * wide), BF16),
            dma((5,)),
            dma((2,)),
            dma((len(ROUTES),)),
            dma((len(RELAYED), PIECES)),
            dma((len(FINAL) + 1,)),
            dma((FAR + 2,)),
            dma((FAR + 2,)),
            dma((4,)),
            dma((4,)),
            dma((1,)),
            dma((chunks,)),
            dma((1,)),
            dma((chunks, 4 if lanes == 2 else levels + 1)),
            pltpu.VMEM((chunks, levels, out_rows, 2 * wide) if lanes == 2 else (1, 1, 8, 128), F32),
            pltpu.VMEM((GIFTS, 2, rows, 2 * wide), BF16),
            pltpu.VMEM((levels, out_rows, 4 * rows) if lanes == 2 else (1, 16, 128), BF16),
            dma((GIFTS, 2)),
            dma((GIFTS, 2)),
            pltpu.VMEM((2, parts, 2, rows, rows // parts), F32),
        ],
        compiler_params=pltpu.CompilerParams(
            collective_id=0, has_side_effects=True, vmem_limit_bytes=56 * 1024 * 1024
        ),
    )(green, direction, partners, counts)
    out = out.reshape(out_rows, half // 128, 2, 128)
    return jnp.swapaxes(out, 1, 2).reshape(out_rows, 2, half)


def solution(mesh):
    in_specs = (
        P(None, ("freq", "tile"), "src"),
        P(None, ("freq", "src"), None),
        P(("freq", "tile"), None),
        P(("freq", "tile")),
    )
    out_specs = P(("freq", "tile"), None, "src")
    body = functools.partial(shards, mesh.shape["tile"])
    return jax.shard_map(body, mesh=mesh, in_specs=in_specs, out_specs=out_specs, check_vma=False)
```

```python
import functools

import jax
import jax.numpy as jnp
from jax import lax
from jax.experimental import pallas as pl
from jax.experimental.pallas import tpu as pltpu
from jax.sharding import PartitionSpec as P

BAND_DEV = 3
PIECES = 8
CHUNKS = 4
SHORT_CHUNKS = 8
GIFTS = 1
PASS_AT = 2
TURN_AT = 4
GIVE_AT = 0
OWN, ACROSS, NEAR, BACK, BACK_ACROSS, NEAR_ACROSS, FAR, PAIR, PAIR_ACROSS, PAIR_END, PAIR_END_ACROSS = range(11)
OFFSETS = (0, 1, 2, -2, -1, 3, -3)
ROUTES = (
    (OWN, ACROSS),
    (OWN, BACK),
    (OWN, NEAR),
    (ACROSS, NEAR_ACROSS),
    (NEAR, BACK_ACROSS),
    (BACK_ACROSS, FAR),
)
RELAYED = (0, 2, 4)
FINAL = (1, 3, 5)
F32 = jnp.float32
BF16 = jnp.bfloat16


def dot(left, right, dims):
    return lax.dot_general(left, right, (dims, ((), ())), preferred_element_type=F32)


def short_line(out_rows, levels):
    return out_rows % 128 == 0 and levels <= 4


def kernel(
    count_tile, a_ref, v_ref, partners_ref, counts_ref, out_ref,
    table, sampled, win, vbuf, img, ipart, irecv, cpart, crecv, acc, w, turned, hp, hr,
    load_sem, img_sem, route_send, relay_recv, final_recv, couple_send, couple_recv,
    pair_send, pair_recv, w_send, w_recv, h_send, h_recv, tot,
    gift, turned_end, gift_send, gift_recv, far_sums,
):
    me = lax.axis_index("tile")
    core = lax.axis_index("src")
    side = lax.rem(me, 2)
    level = me // 2
    levels = count_tile // 2
    step = 1 - 2 * side
    rows, half = win.shape[2], win.shape[3]
    tiles, kmax = table.shape
    out_rows = out_ref.shape[0]
    chunks, wide = w.shape[0], w.shape[3] // 2

    def inside(place):
        return (place >= 0) & (place < levels)

    has_near = inside(level + step)
    has_back = inside(level - step)
    has_far = inside(level - 2 * step)
    across = {"tile": me + step}
    forward = {"tile": me + 2 * step}
    backward = {"tile": me - 2 * step}
    partner = {"src": 1 - core}
    targets = (across, forward, backward, backward, across, forward)
    sends = (None, has_near, has_back, has_back, has_near, has_near & has_back)
    arrives = (None, has_back, has_near, has_near, has_back, has_far)

    ends = short_line(out_rows, levels) and levels == 4
    given = chunks - gift.shape[0] if ends else chunks
    gives = (level == 0) | (level == levels - 1)
    takes = (level == 1) | (level == levels - 2)
    giver = jnp.where(level == 1, 0, levels - 1)
    end_near = giver == level + step
    end_slot = jnp.where(end_near, NEAR, BACK)
    end_across = jnp.where(end_near, NEAR_ACROSS, BACK_ACROSS)

    def guarded(condition, run):
        if condition is None:
            run()
        else:
            pl.when(condition)(run)

    def remote(source, target, send, recv, device):
        return pltpu.make_async_remote_copy(
            src_ref=source, dst_ref=target, send_sem=send, recv_sem=recv,
            device_id=device, device_id_type=pl.DeviceIdType.MESH,
        )

    depth = rows // PIECES
    parts = 2 if rows % 256 == 0 else 1

    def piece(slot, index, count=1):
        return win.at[slot, :, pl.ds(index * depth, count * depth)]

    def route(number, index, count=1):
        source, target = ROUTES[number]
        if number in RELAYED:
            recv = relay_recv.at[RELAYED.index(number), index]
        else:
            recv = final_recv.at[FINAL.index(number) + (index * parts // PIECES if number == 5 else 0)]
        return remote(
            piece(source, index, count), piece(target, index, count), route_send.at[number], recv, targets[number]
        )

    def send_route(number, index):
        guarded(sends[number], lambda: route(number, index).start())

    def arrive(number, index, count=1):
        guarded(arrives[number], lambda: route(number, index, count).wait_recv())

    def to_pair(source, target, number):
        return remote(win.at[source], win.at[target], pair_send.at[number], pair_recv.at[number], partner)

    load_a = pltpu.make_async_copy(a_ref, win.at[OWN], load_sem.at[0])
    load_theirs = pltpu.make_async_copy(
        v_ref.at[:, :, pl.ds(pl.multiple_of((1 - core) * half, half), half)], vbuf.at[0], load_sem.at[1]
    )
    load_mine = pltpu.make_async_copy(
        v_ref.at[:, :, pl.ds(pl.multiple_of(core * half, half), half)], vbuf.at[1], load_sem.at[2]
    )
    load_table = pltpu.make_async_copy(partners_ref, table, load_sem.at[3])
    load_counts = pltpu.make_async_copy(counts_ref, sampled, load_sem.at[4])
    load_a.start()
    def later_loads():
        load_theirs.start()
        load_mine.start()
        load_table.start()
        load_counts.start()

    barrier = pltpu.get_barrier_semaphore()
    pl.semaphore_signal(barrier, inc=1, device_id=partner, device_id_type=pl.DeviceIdType.MESH)
    pl.semaphore_signal(barrier, inc=1, device_id=across, device_id_type=pl.DeviceIdType.MESH)

    def other_level(number):
        return lax.rem(level + 1 + number, levels)

    if short_line(out_rows, levels):
        for there, device in ((has_near, forward), (has_back, backward)):
            @pl.when(there)
            def _(device=device):
                pl.semaphore_signal(barrier, inc=1, device_id=device, device_id_type=pl.DeviceIdType.MESH)

        later_loads()
        pl.semaphore_wait(barrier, 2 + has_near.astype(jnp.int32) + has_back.astype(jnp.int32))
    else:
        @pl.loop(0, levels - 1)
        def _(number):
            pl.semaphore_signal(
                barrier, inc=1, device_id={"tile": other_level(number) * 2 + side},
                device_id_type=pl.DeviceIdType.MESH,
            )

        later_loads()
        pl.semaphore_wait(barrier, levels + 1)
    load_a.wait()
    for index in range(PIECES):
        for number in (0, 1, 2):
            send_route(number, index)
    to_pair(OWN, PAIR, 0).start()

    own = win[OWN].reshape(2 * rows, half)

    def images(slot):
        first = dot(own, vbuf[slot, 0], ((1,), (0,)))
        second = dot(own, vbuf[slot, 1], ((1,), (0,)))
        return first[:rows] - second[rows:], second[:rows] + first[rows:]

    load_theirs.wait()
    real, imag = images(0)
    ipart[0] = real
    ipart[1] = imag
    image_copy = remote(ipart, irecv, img_sem.at[0], img_sem.at[1], partner)
    image_copy.start()
    load_mine.wait()
    real, imag = images(1)
    image_copy.wait_recv()
    img[:rows] = (real + irecv[0]).astype(BF16)
    img[rows:] = (imag + irecv[1]).astype(BF16)

    load_table.wait()
    load_counts.wait()
    acc[...] = jnp.zeros_like(acc)

    def exists(slot):
        return (
            (slot <= ACROSS)
            | (((slot == NEAR) | (slot == NEAR_ACROSS)) & has_near)
            | (((slot == BACK) | (slot == BACK_ACROSS)) & has_back)
            | ((slot == FAR) & has_far)
        )

    def sample(slot):
        offset = 0
        for index, value in enumerate(OFFSETS):
            offset = jnp.where(slot == index, value, offset)
        first = (me + offset * step) * tiles
        tile = rows // tiles
        bands = []
        for row in range(tiles):
            blocks = []
            for column in range(tiles):
                hit = False
                for k in range(kmax):
                    hit = hit | ((table[row, k] == first + column) & (k < sampled[row]))
                blocks.append(jnp.full((tile, tile), jnp.where(hit, 1.0, 0.0), F32))
            bands.append(jnp.concatenate(blocks, axis=1))
        return jnp.concatenate(bands, axis=0)

    def couple_copy(slot):
        return remote(cpart.at[slot], crecv.at[slot], couple_send.at[slot], couple_recv.at[slot], partner)

    def couple(low, high):
        @pl.loop(low, high)
        def _(slot):
            @pl.when(exists(slot))
            def _():
                block = win[slot].reshape(2 * rows, half)
                prod = dot(img[...], block, ((1,), (1,)))
                cpart[slot, 0] = prod[:rows, :rows] + prod[rows:, rows:]
                cpart[slot, 1] = prod[rows:, :rows] - prod[:rows, rows:]
                couple_copy(slot).start()

    def weigh(low, high):
        @pl.loop(low, high)
        def _(slot):
            @pl.when(exists(slot))
            def _():
                couple_copy(slot).wait_recv()
                live = sample(slot)
                real = ((cpart[slot, 0] + crecv[slot, 0]) * live).astype(BF16)
                imag = ((cpart[slot, 1] + crecv[slot, 1]) * live).astype(BF16)
                left = jnp.concatenate(
                    [jnp.concatenate([real, -imag], axis=1), jnp.concatenate([imag, real], axis=1)], axis=0
                )
                acc[...] += dot(left, win[slot].reshape(2 * rows, half), ((1,), (0,)))

    def pass_on(index):
        arrive(0, index)
        send_route(3, index)
        arrive(2, index)
        send_route(4, index)

    couple(OWN, ACROSS)
    for index in range(PIECES):
        pass_on(index)
    to_pair(ACROSS, PAIR_ACROSS, 1).start()
    arrive(1, 0, PIECES)
    if ends:
        pl.when(takes)(lambda: to_pair(end_slot, PAIR_END, 2).start())
    span = max(out_rows, 128)

    def lay(target, group, block, slot, lanes):
        for part in range(2):
            first = (2 * block + part) * rows
            target[group, :, first : first + rows] = win[slot, part, :, lanes].T

    def turn_over():
        to_pair(OWN, PAIR, 0).wait_recv()
        to_pair(ACROSS, PAIR_ACROSS, 1).wait_recv()

        @pl.loop(0, turned.shape[0])
        def _(group):
            column = (2 * group + side) * out_rows if span == out_rows else group * span
            which = column // half
            base = jnp.where(which == core, OWN, PAIR)
            lanes = pl.ds(pl.multiple_of(column - which * half, 128), span)
            for block in range(2):
                lay(turned, group, block, base + block, lanes)

    jobs = (
        lambda: couple(ACROSS, BACK_ACROSS),
        lambda: weigh(OWN, NEAR),
        lambda: weigh(NEAR, BACK_ACROSS),
        turn_over,
    )
    for index in range(PIECES):
        for job in jobs[index * len(jobs) // PIECES : (index + 1) * len(jobs) // PIECES]:
            job()
        arrive(4, index)
        send_route(5, index)
    couple(BACK_ACROSS, NEAR_ACROSS)
    arrive(3, 0, PIECES)
    couple(NEAR_ACROSS, FAR)
    part_rows = rows // parts

    def far_part(part):
        return win[FAR, :, part * part_rows : (part + 1) * part_rows].reshape(2 * part_rows, half)

    def far_copy(part):
        return remote(
            far_sums.at[0, part], far_sums.at[1, part],
            couple_send.at[FAR + part], couple_recv.at[FAR + part], partner,
        )

    def couple_far(part):
        @pl.when(has_far)
        def _():
            arrive_far(part)
            prod = dot(img[...], far_part(part), ((1,), (1,)))
            for index, value in enumerate((
                prod[:rows, :part_rows] + prod[rows:, part_rows:],
                prod[rows:, :part_rows] - prod[:rows, part_rows:],
            )):
                far_sums[0, part, index] = value
            far_copy(part).start()

    def arrive_far(part):
        route(5, part * PIECES // parts, PIECES // parts).wait_recv()

    def weigh_far(part):
        @pl.when(has_far)
        def _():
            far_copy(part).wait_recv()
            columns = slice(part * part_rows, (part + 1) * part_rows)
            live = sample(FAR)[:, columns]
            real = ((far_sums[0, part, 0] + far_sums[1, part, 0]) * live).astype(BF16)
            imag = ((far_sums[0, part, 1] + far_sums[1, part, 1]) * live).astype(BF16)
            left = jnp.concatenate(
                [jnp.concatenate([real, -imag], axis=1), jnp.concatenate([imag, real], axis=1)], axis=0
            )
            acc[...] += dot(left, far_part(part), ((1,), (0,)))

    couple_far(0)
    weigh(BACK_ACROSS, FAR)
    for part in range(1, parts):
        couple_far(part)
        weigh_far(part - 1)
    weigh_far(parts - 1)

    def w_copy(chunk):
        return remote(w.at[chunk, 0], w.at[chunk, 1], w_send.at[0], w_recv.at[chunk], across)

    def halves(first, second):
        low = lax.broadcasted_iota(jnp.int32, first.shape, 1) < wide
        return (
            jnp.where(low, first, pltpu.roll(second, wide, 1)),
            jnp.where(low, pltpu.roll(first, wide, 1), second),
        )

    def gift_copy(index, hop):
        source = w.at[given + index, 0] if hop == 0 else gift.at[index, 0]
        device = {"tile": me + jnp.where(level == 0, 2, -2)} if hop == 0 else across
        return remote(
            source, gift.at[index, hop], gift_send.at[index, hop], gift_recv.at[index, hop], device
        )

    span_chunks = 2 if wide % 128 else 1
    for first in range(0, chunks, span_chunks):
        columns = slice(first * wide, (first + span_chunks) * wide)
        real, imag = acc[:rows, columns], acc[rows:, columns]
        if wide % 128:
            packed = halves(real, imag)
        else:
            packed = (jnp.concatenate([real, imag], axis=1),)
        for index, value in enumerate(packed):
            w[first + index, 0] = value.astype(BF16)
            w_copy(first + index).start()

    def give(when):
        @pl.when(gives & when)
        def _():
            for index in range(chunks - given):
                gift_copy(index, 0).start()

    if ends:
        give(jnp.logical_not(has_far))

        pl.when(takes)(lambda: to_pair(end_across, PAIR_END_ACROSS, 3).start())

    def turn_end():
        @pl.when(takes)
        def _():
            to_pair(end_slot, PAIR_END, 2).wait_recv()
            to_pair(end_across, PAIR_END_ACROSS, 3).wait_recv()
            for group in range(levels):
                column = (2 * group + side) * out_rows
                which = column // half
                lanes = pl.ds(pl.multiple_of(column - which * half, 128), span)
                for block, (here, there) in enumerate(((end_slot, PAIR_END), (end_across, PAIR_END_ACROSS))):
                    lay(turned_end, group, block, jnp.where(which == core, here, there), lanes)

    def product(left, right):
        depth = left.shape[1] // 2
        straight = dot(left[:, :depth], right, ((1,), (0,)))
        crossed = pltpu.roll(dot(left[:, depth:], right, ((1,), (0,))), wide, 1)
        low = lax.broadcasted_iota(jnp.int32, crossed.shape, 1) < wide
        return straight + jnp.where(low, crossed, -crossed)

    def block_product(left, block, right):
        every = left[:, :, block * 2 * rows : (block + 1) * 2 * rows].reshape(levels * out_rows, 2 * rows)
        return product(every, right).reshape(levels, out_rows, 2 * wide)

    def partial(chunk, group):
        left = turned[group]
        return product(left[:, : 2 * rows], w[chunk, 0]) + product(left[:, 2 * rows :], w[chunk, 1])

    def rows_of(target):
        return pl.multiple_of((2 * target + side) * out_rows, out_rows)

    def put(chunk, total):
        for part in range(2):
            for index in range(wide // 128):
                first = part * wide + index * 128
                out_ref[:, 2 * (chunk * wide // 128 + index) + part] = total[:, first : first + 128]

    def term(chunk, lane, slot, target, level_to, arrival=None):
        return remote(
            hp.at[chunk, pl.ds(rows_of(target), out_rows)], hr.at[chunk, lane, slot],
            h_send.at[0], h_recv.at[chunk, slot if arrival is None else arrival], {"tile": 2 * level_to + side},
        )

    def settle():
        for number in range(len(ROUTES)):
            guarded(sends[number], lambda number=number: route(number, 0, PIECES).wait_send())
        to_pair(OWN, PAIR, 0).wait_send()
        to_pair(ACROSS, PAIR_ACROSS, 1).wait_send()
        image_copy.wait_send()

        @pl.loop(0, FAR)
        def _(slot):
            @pl.when(exists(slot))
            def _():
                couple_copy(slot).wait_send()

        @pl.when(has_far)
        def _():
            for part in range(parts):
                far_copy(part).wait_send()

        if ends:
            @pl.when(gives)
            def _():
                for index in range(chunks - given):
                    gift_copy(index, 0).wait_send()

            @pl.when(takes)
            def _():
                for index in range(chunks - given):
                    gift_copy(index, 1).wait_send()
                to_pair(end_slot, PAIR_END, 2).wait_send()
                to_pair(end_across, PAIR_END_ACROSS, 3).wait_send()

        remote(w.at[:, 0], w.at[:, 1], w_send.at[0], w_recv.at[0], across).wait_send()

        def sent(count):
            rows_sent = hp.at[:count, pl.ds(0, (levels - 1) * out_rows)]
            remote(rows_sent, rows_sent, h_send.at[0], h_recv.at[0, 0], across).wait_send()

        if levels > 1:
            if given == chunks:
                sent(chunks)
            else:
                pl.when(gives)(lambda: sent(given))
                pl.when(takes)(lambda: sent(chunks))

    if short_line(out_rows, levels):
        depths = level, levels - 1 - level

        def total(chunk):
            tot[chunk] = block_product(turned, 0, w[chunk, 0])
            w_copy(chunk).wait_recv()
            tot[chunk] += block_product(turned, 1, w[chunk, 1])

        def place(target):
            return pl.ds(rows_of(target), out_rows)

        def far(lane, number):
            return levels - 1 - number if lane == 0 else number

        def passing(chunk, lane, target, number):
            arrival = number if number < levels - 2 else 2 + lane
            return term(chunk, lane, target, target, level + 1 - 2 * lane, arrival)

        def begin(chunk, numbers):
            for lane in range(2):
                for number in numbers:
                    target = far(lane, number)

                    @pl.when(depths[lane] == 0)
                    def _(lane=lane, target=target, number=number):
                        hp[chunk, place(target)] = tot[chunk, target].astype(BF16)
                        passing(chunk, lane, target, number).start()

        def beside(chunk):
            for lane in range(2):
                target = far(lane, 0)

                @pl.when(depths[lane] == 2)
                def _(lane=lane, target=target):
                    hp[chunk, place(target)] = tot[chunk, target].astype(BF16)
                    term(chunk, lane, levels, target, target, 0).start()

        def add_on(chunk, number):
            for lane in range(2):
                target = far(lane, number)

                @pl.when(depths[lane] == 1)
                def _(lane=lane, target=target):
                    value = tot[chunk, target]
                    if chunk < given:
                        passing(chunk, lane, target, number).wait_recv()
                        value = value + hr[chunk, lane, target].astype(F32)
                    hp[chunk, place(target)] = value.astype(BF16)
                    term(chunk, lane, target, target, target, 2 + lane).start()

        def pass_gift(index):
            @pl.when(takes)
            def _():
                gift_copy(index, 0).wait_recv()
                gift_copy(index, 1).start()

        def use_gift(index, block):
            @pl.when(takes)
            def _():
                if block:
                    gift_copy(index, 1).wait_recv()
                more = block_product(turned_end, block, gift[index, block])
                for target in range(1, levels - 1):
                    tot[given + index, target] += more[target]
                far_end = jnp.where(level == 1, levels - 1, 0)
                tot[given + index, far_end] += jnp.where(level == 1, more[levels - 1], more[0])

        distant = range(levels - 2)

        for chunk in range(chunks + 1):
            if chunk < chunks:
                total(chunk)
                if chunk < given:
                    begin(chunk, distant)
                if levels > 3:
                    beside(chunk)
            if ends and chunk == GIVE_AT:
                give(has_far)
            if chunk == given - 1 and levels > 1:
                for done in range(given):
                    begin(done, (levels - 2,))
            if ends and chunk == TURN_AT:
                turn_end()
            if 0 <= chunk - PASS_AT < chunks - given:
                pass_gift(chunk - PASS_AT)
            if ends and chunk == given:
                use_gift(0, 0)
                add_on(chunk - 1, 0)
                use_gift(0, 1)
                for number, done in ((0, chunk), (1, chunk - 1), (1, chunk)):
                    add_on(done, number)
            elif 0 < chunk < given or given == chunks == chunk:
                for number in distant:
                    add_on(chunk - 1, number)

        for chunk in range(chunks):
            if chunk == chunks - 1:
                settle()
            for lane, slot, arrival, there in (
                (0, level, 2, depths[0] > (1 if chunk >= given else 0)),
                (1, level, 3, depths[1] > (1 if chunk >= given else 0)),
                (0, levels, 0, depths[0] > 2), (1, levels, 0, depths[1] > 2),
            ):
                @pl.when(there)
                def _(chunk=chunk, lane=lane, slot=slot, arrival=arrival):
                    term(chunk, lane, slot, level, level, arrival).wait_recv()
                    tot[chunk, level] += hr[chunk, lane, slot].astype(F32)
            if wide % 128 == 0:
                put(chunk, tot[chunk, level])
            elif chunk % 2:
                for part, value in enumerate(halves(tot[chunk - 1, level], tot[chunk, level])):
                    out_ref[:, chunk - 1 + part] = value
    else:
        for chunk in range(chunks):
            w_copy(chunk).wait_recv()
            if span != out_rows:
                @pl.loop(0, hp.shape[1] // span)
                def _(group):
                    column = pl.multiple_of(group * span, span)
                    hp[chunk, pl.ds(column, span)] = partial(chunk, group).astype(BF16)

            @pl.loop(0, levels - 1)
            def _(number):
                target = other_level(number)
                if span == out_rows:
                    hp[chunk, pl.ds(rows_of(target), out_rows)] = partial(chunk, target).astype(BF16)
                term(chunk, 0, level, target, target).start()

            if span == out_rows:
                hp[chunk, pl.ds(rows_of(level), out_rows)] = partial(chunk, level).astype(BF16)

        for chunk in range(chunks):
            def add(number, total):
                sender = other_level(number)
                term(chunk, 0, sender, level, sender).wait_recv()
                return total + hr[chunk, 0, sender].astype(F32)

            put(chunk, lax.fori_loop(0, levels - 1, add, hp[chunk, pl.ds(rows_of(level), out_rows)].astype(F32)))

        settle()

def shards(count_tile, green, direction, partners, counts):
    tile_dev, kmax = partners.shape
    rows, half = green.shape[1:]
    sources = direction.shape[2]
    out_rows = sources // count_tile
    levels = count_tile // 2
    chunks = SHORT_CHUNKS if short_line(out_rows, levels) else CHUNKS
    wide = half // chunks
    parts = 2 if rows % 256 == 0 else 1
    lanes = 2 if short_line(out_rows, levels) else 1
    anywhere = pl.BlockSpec(memory_space=pl.ANY)
    local = pl.BlockSpec(memory_space=pltpu.VMEM)
    dma = pltpu.SemaphoreType.DMA
    out = pl.pallas_call(
        functools.partial(kernel, count_tile),
        out_shape=jax.ShapeDtypeStruct((out_rows, half // 64, 128), F32),
        in_specs=[anywhere] * 4,
        out_specs=local,
        scratch_shapes=[
            pltpu.SMEM((tile_dev, kmax), jnp.int32),
            pltpu.SMEM((tile_dev,), jnp.int32),
            pltpu.VMEM((PAIR_END_ACROSS + 1, 2, rows, half), BF16),
            pltpu.VMEM((2, 2, half, half), BF16),
            pltpu.VMEM((2 * rows, half), BF16),
            pltpu.VMEM((2, rows, half), F32),
            pltpu.VMEM((2, rows, half), F32),
            pltpu.VMEM((FAR, 2, rows, rows), F32),
            pltpu.VMEM((FAR, 2, rows, rows), F32),
            pltpu.VMEM((2 * rows, half), F32),
            pltpu.VMEM((chunks, 2, rows, 2 * wide), BF16),
            pltpu.VMEM((levels if out_rows >= 128 else sources // 128, max(out_rows, 128), 4 * rows), BF16),
            pltpu.VMEM((chunks, sources, 2 * wide), BF16),
            pltpu.VMEM((chunks, lanes, levels + 1, out_rows, 2 * wide), BF16),
            dma((5,)),
            dma((2,)),
            dma((len(ROUTES),)),
            dma((len(RELAYED), PIECES)),
            dma((len(FINAL) + 1,)),
            dma((FAR + 2,)),
            dma((FAR + 2,)),
            dma((4,)),
            dma((4,)),
            dma((1,)),
            dma((chunks,)),
            dma((1,)),
            dma((chunks, 4 if lanes == 2 else levels + 1)),
            pltpu.VMEM((chunks, levels, out_rows, 2 * wide) if lanes == 2 else (1, 1, 8, 128), F32),
            pltpu.VMEM((GIFTS, 2, rows, 2 * wide), BF16),
            pltpu.VMEM((levels, out_rows, 4 * rows) if lanes == 2 else (1, 16, 128), BF16),
            dma((GIFTS, 2)),
            dma((GIFTS, 2)),
            pltpu.VMEM((2, parts, 2, rows, rows // parts), F32),
        ],
        compiler_params=pltpu.CompilerParams(
            collective_id=0, has_side_effects=True, vmem_limit_bytes=56 * 1024 * 1024
        ),
    )(green, direction, partners, counts)
    out = out.reshape(out_rows, half // 128, 2, 128)
    return jnp.swapaxes(out, 1, 2).reshape(out_rows, 2, half)


def solution(mesh):
    in_specs = (
        P(None, ("freq", "tile"), "src"),
        P(None, ("freq", "src"), None),
        P(("freq", "tile"), None),
        P(("freq", "tile")),
    )
    out_specs = P(("freq", "tile"), None, "src")
    body = functools.partial(shards, mesh.shape["tile"])
    return jax.shard_map(body, mesh=mesh, in_specs=in_specs, out_specs=out_specs, check_vma=False)
```

```python
import functools

import jax
import jax.numpy as jnp
from jax import lax
from jax.experimental import pallas as pl
from jax.experimental.pallas import tpu as pltpu
from jax.sharding import PartitionSpec as P

BAND_DEV = 3
PIECES = 8
CHUNKS = 4
SHORT_CHUNKS = 8
GIFTS = 1
PASS_AT = 2
TURN_AT = 4
GIVE_AT = 0
OWN, ACROSS, NEAR, BACK, BACK_ACROSS, NEAR_ACROSS, FAR, PAIR, PAIR_ACROSS, PAIR_END, PAIR_END_ACROSS = range(11)
OFFSETS = (0, 1, 2, -2, -1, 3, -3)
ROUTES = (
    (OWN, ACROSS),
    (OWN, BACK),
    (OWN, NEAR),
    (ACROSS, NEAR_ACROSS),
    (NEAR, BACK_ACROSS),
    (BACK_ACROSS, FAR),
)
RELAYED = (0, 2, 4)
FINAL = (1, 3, 5)
F32 = jnp.float32
BF16 = jnp.bfloat16


def dot(left, right, dims):
    return lax.dot_general(left, right, (dims, ((), ())), preferred_element_type=F32)


def short_line(out_rows, levels):
    return out_rows % 128 == 0 and levels <= 4


def kernel(
    count_tile, a_ref, v_ref, partners_ref, counts_ref, out_ref,
    table, sampled, win, vbuf, img, ipart, irecv, cpart, crecv, acc, w, turned, hp, hr,
    load_sem, img_sem, route_send, relay_recv, final_recv, couple_send, couple_recv,
    pair_send, pair_recv, w_send, w_recv, h_send, h_recv, tot,
    gift, turned_end, gift_send, gift_recv, far_sums,
):
    me = lax.axis_index("tile")
    core = lax.axis_index("src")
    side = lax.rem(me, 2)
    level = me // 2
    levels = count_tile // 2
    step = 1 - 2 * side
    rows, half = win.shape[2], win.shape[3]
    tiles, kmax = table.shape
    out_rows = out_ref.shape[0]
    chunks, wide = w.shape[0], w.shape[3] // 2

    def inside(place):
        return (place >= 0) & (place < levels)

    has_near = inside(level + step)
    has_back = inside(level - step)
    has_far = inside(level - 2 * step)
    across = {"tile": me + step}
    forward = {"tile": me + 2 * step}
    backward = {"tile": me - 2 * step}
    partner = {"src": 1 - core}
    targets = (across, forward, backward, backward, across, forward)
    sends = (None, has_near, has_back, has_back, has_near, has_near & has_back)
    arrives = (None, has_back, has_near, has_near, has_back, has_far)

    ends = short_line(out_rows, levels) and levels == 4
    given = chunks - gift.shape[0] if ends else chunks
    gives = (level == 0) | (level == levels - 1)
    takes = (level == 1) | (level == levels - 2)
    giver = jnp.where(level == 1, 0, levels - 1)
    end_near = giver == level + step
    end_slot = jnp.where(end_near, NEAR, BACK)
    end_across = jnp.where(end_near, NEAR_ACROSS, BACK_ACROSS)

    def guarded(condition, run):
        if condition is None:
            run()
        else:
            pl.when(condition)(run)

    def remote(source, target, send, recv, device):
        return pltpu.make_async_remote_copy(
            src_ref=source, dst_ref=target, send_sem=send, recv_sem=recv,
            device_id=device, device_id_type=pl.DeviceIdType.MESH,
        )

    depth = rows // PIECES
    parts = 2 if rows % 256 == 0 else 1

    def piece(slot, index, count=1):
        return win.at[slot, :, pl.ds(index * depth, count * depth)]

    def route(number, index, count=1):
        source, target = ROUTES[number]
        if number in RELAYED:
            recv = relay_recv.at[RELAYED.index(number), index]
        else:
            recv = final_recv.at[FINAL.index(number) + (index * parts // PIECES if number == 5 else 0)]
        return remote(
            piece(source, index, count), piece(target, index, count), route_send.at[number], recv, targets[number]
        )

    def send_route(number, index):
        guarded(sends[number], lambda: route(number, index).start())

    def arrive(number, index, count=1):
        guarded(arrives[number], lambda: route(number, index, count).wait_recv())

    def to_pair(source, target, number):
        return remote(win.at[source], win.at[target], pair_send.at[number], pair_recv.at[number], partner)

    load_a = pltpu.make_async_copy(a_ref, win.at[OWN], load_sem.at[0])
    load_theirs = pltpu.make_async_copy(
        v_ref.at[:, :, pl.ds(pl.multiple_of((1 - core) * half, half), half)], vbuf.at[0], load_sem.at[1]
    )
    load_mine = pltpu.make_async_copy(
        v_ref.at[:, :, pl.ds(pl.multiple_of(core * half, half), half)], vbuf.at[1], load_sem.at[2]
    )
    load_table = pltpu.make_async_copy(partners_ref, table, load_sem.at[3])
    load_counts = pltpu.make_async_copy(counts_ref, sampled, load_sem.at[4])
    load_a.start()
    def later_loads():
        load_theirs.start()
        load_mine.start()
        load_table.start()
        load_counts.start()

    barrier = pltpu.get_barrier_semaphore()
    pl.semaphore_signal(barrier, inc=1, device_id=partner, device_id_type=pl.DeviceIdType.MESH)
    pl.semaphore_signal(barrier, inc=1, device_id=across, device_id_type=pl.DeviceIdType.MESH)

    def other_level(number):
        return lax.rem(level + 1 + number, levels)

    if short_line(out_rows, levels):
        for there, device in ((has_near, forward), (has_back, backward)):
            @pl.when(there)
            def _(device=device):
                pl.semaphore_signal(barrier, inc=1, device_id=device, device_id_type=pl.DeviceIdType.MESH)

        later_loads()
        pl.semaphore_wait(barrier, 2 + has_near.astype(jnp.int32) + has_back.astype(jnp.int32))
    else:
        @pl.loop(0, levels - 1)
        def _(number):
            pl.semaphore_signal(
                barrier, inc=1, device_id={"tile": other_level(number) * 2 + side},
                device_id_type=pl.DeviceIdType.MESH,
            )

        later_loads()
        pl.semaphore_wait(barrier, levels + 1)
    load_a.wait()
    for index in range(PIECES):
        for number in (0, 1, 2):
            send_route(number, index)
    to_pair(OWN, PAIR, 0).start()

    own = win[OWN].reshape(2 * rows, half)

    def images(slot):
        first = dot(own, vbuf[slot, 0], ((1,), (0,)))
        second = dot(own, vbuf[slot, 1], ((1,), (0,)))
        return first[:rows] - second[rows:], second[:rows] + first[rows:]

    load_theirs.wait()
    real, imag = images(0)
    ipart[0] = real
    ipart[1] = imag
    image_copy = remote(ipart, irecv, img_sem.at[0], img_sem.at[1], partner)
    image_copy.start()
    load_mine.wait()
    real, imag = images(1)
    image_copy.wait_recv()
    img[:rows] = (real + irecv[0]).astype(BF16)
    img[rows:] = (imag + irecv[1]).astype(BF16)

    load_table.wait()
    load_counts.wait()
    acc[...] = jnp.zeros_like(acc)

    def exists(slot):
        return (
            (slot <= ACROSS)
            | (((slot == NEAR) | (slot == NEAR_ACROSS)) & has_near)
            | (((slot == BACK) | (slot == BACK_ACROSS)) & has_back)
            | ((slot == FAR) & has_far)
        )

    def sample(slot):
        offset = 0
        for index, value in enumerate(OFFSETS):
            offset = jnp.where(slot == index, value, offset)
        first = (me + offset * step) * tiles
        tile = rows // tiles
        bands = []
        for row in range(tiles):
            blocks = []
            for column in range(tiles):
                hit = False
                for k in range(kmax):
                    hit = hit | ((table[row, k] == first + column) & (k < sampled[row]))
                blocks.append(jnp.full((tile, tile), jnp.where(hit, 1.0, 0.0), F32))
            bands.append(jnp.concatenate(blocks, axis=1))
        return jnp.concatenate(bands, axis=0)

    def couple_copy(slot):
        return remote(cpart.at[slot], crecv.at[slot], couple_send.at[slot], couple_recv.at[slot], partner)

    def couple(low, high):
        @pl.loop(low, high)
        def _(slot):
            @pl.when(exists(slot))
            def _():
                block = win[slot].reshape(2 * rows, half)
                prod = dot(img[...], block, ((1,), (1,)))
                cpart[slot, 0] = prod[:rows, :rows] + prod[rows:, rows:]
                cpart[slot, 1] = prod[rows:, :rows] - prod[:rows, rows:]
                couple_copy(slot).start()

    def weigh(low, high):
        @pl.loop(low, high)
        def _(slot):
            @pl.when(exists(slot))
            def _():
                couple_copy(slot).wait_recv()
                live = sample(slot)
                real = ((cpart[slot, 0] + crecv[slot, 0]) * live).astype(BF16)
                imag = ((cpart[slot, 1] + crecv[slot, 1]) * live).astype(BF16)
                left = jnp.concatenate(
                    [jnp.concatenate([real, -imag], axis=1), jnp.concatenate([imag, real], axis=1)], axis=0
                )
                acc[...] += dot(left, win[slot].reshape(2 * rows, half), ((1,), (0,)))

    def pass_on(index):
        arrive(0, index)
        send_route(3, index)
        arrive(2, index)
        send_route(4, index)

    couple(OWN, ACROSS)
    for index in range(PIECES):
        pass_on(index)
    to_pair(ACROSS, PAIR_ACROSS, 1).start()
    arrive(1, 0, PIECES)
    if ends:
        pl.when(takes)(lambda: to_pair(end_slot, PAIR_END, 2).start())
    span = max(out_rows, 128)

    def lay(target, group, block, slot, lanes):
        for part in range(2):
            first = (2 * block + part) * rows
            target[group, :, first : first + rows] = win[slot, part, :, lanes].T

    def turn_over():
        to_pair(OWN, PAIR, 0).wait_recv()
        to_pair(ACROSS, PAIR_ACROSS, 1).wait_recv()

        @pl.loop(0, turned.shape[0])
        def _(group):
            column = (2 * group + side) * out_rows if span == out_rows else group * span
            which = column // half
            base = jnp.where(which == core, OWN, PAIR)
            lanes = pl.ds(pl.multiple_of(column - which * half, 128), span)
            for block in range(2):
                lay(turned, group, block, base + block, lanes)

    jobs = (
        lambda: couple(ACROSS, BACK_ACROSS),
        lambda: weigh(OWN, NEAR),
        lambda: weigh(NEAR, BACK_ACROSS),
        turn_over,
    )
    for index in range(PIECES):
        for job in jobs[index * len(jobs) // PIECES : (index + 1) * len(jobs) // PIECES]:
            job()
        arrive(4, index)
        send_route(5, index)
    couple(BACK_ACROSS, NEAR_ACROSS)
    arrive(3, 0, PIECES)
    couple(NEAR_ACROSS, FAR)
    part_rows = rows // parts

    def far_part(part):
        return win[FAR, :, part * part_rows : (part + 1) * part_rows].reshape(2 * part_rows, half)

    def far_copy(part):
        return remote(
            far_sums.at[0, part], far_sums.at[1, part],
            couple_send.at[FAR + part], couple_recv.at[FAR + part], partner,
        )

    def couple_far(part):
        @pl.when(has_far)
        def _():
            arrive_far(part)
            prod = dot(img[...], far_part(part), ((1,), (1,)))
            for index, value in enumerate((
                prod[:rows, :part_rows] + prod[rows:, part_rows:],
                prod[rows:, :part_rows] - prod[:rows, part_rows:],
            )):
                far_sums[0, part, index] = value
            far_copy(part).start()

    def arrive_far(part):
        route(5, part * PIECES // parts, PIECES // parts).wait_recv()

    def weigh_far(part):
        @pl.when(has_far)
        def _():
            far_copy(part).wait_recv()
            columns = slice(part * part_rows, (part + 1) * part_rows)
            live = sample(FAR)[:, columns]
            real = ((far_sums[0, part, 0] + far_sums[1, part, 0]) * live).astype(BF16)
            imag = ((far_sums[0, part, 1] + far_sums[1, part, 1]) * live).astype(BF16)
            left = jnp.concatenate(
                [jnp.concatenate([real, -imag], axis=1), jnp.concatenate([imag, real], axis=1)], axis=0
            )
            acc[...] += dot(left, far_part(part), ((1,), (0,)))

    couple_far(0)
    pl.when(core == 0)(lambda: weigh(BACK_ACROSS, FAR))
    for part in range(1, parts):
        couple_far(part)
    pl.when(core != 0)(lambda: weigh(BACK_ACROSS, FAR))
    for part in range(parts):
        weigh_far(part)

    def w_copy(chunk):
        return remote(w.at[chunk, 0], w.at[chunk, 1], w_send.at[0], w_recv.at[chunk], across)

    def halves(first, second):
        low = lax.broadcasted_iota(jnp.int32, first.shape, 1) < wide
        return (
            jnp.where(low, first, pltpu.roll(second, wide, 1)),
            jnp.where(low, pltpu.roll(first, wide, 1), second),
        )

    def gift_copy(index, hop):
        source = w.at[given + index, 0] if hop == 0 else gift.at[index, 0]
        device = {"tile": me + jnp.where(level == 0, 2, -2)} if hop == 0 else across
        return remote(
            source, gift.at[index, hop], gift_send.at[index, hop], gift_recv.at[index, hop], device
        )

    span_chunks = 2 if wide % 128 else 1
    for first in range(0, chunks, span_chunks):
        columns = slice(first * wide, (first + span_chunks) * wide)
        real, imag = acc[:rows, columns], acc[rows:, columns]
        if wide % 128:
            packed = halves(real, imag)
        else:
            packed = (jnp.concatenate([real, imag], axis=1),)
        for index, value in enumerate(packed):
            w[first + index, 0] = value.astype(BF16)
            w_copy(first + index).start()

    def give(when):
        @pl.when(gives & when)
        def _():
            for index in range(chunks - given):
                gift_copy(index, 0).start()

    if ends:
        give(jnp.logical_not(has_far))

        pl.when(takes)(lambda: to_pair(end_across, PAIR_END_ACROSS, 3).start())

    def turn_end():
        @pl.when(takes)
        def _():
            to_pair(end_slot, PAIR_END, 2).wait_recv()
            to_pair(end_across, PAIR_END_ACROSS, 3).wait_recv()
            for group in range(levels):
                column = (2 * group + side) * out_rows
                which = column // half
                lanes = pl.ds(pl.multiple_of(column - which * half, 128), span)
                for block, (here, there) in enumerate(((end_slot, PAIR_END), (end_across, PAIR_END_ACROSS))):
                    lay(turned_end, group, block, jnp.where(which == core, here, there), lanes)

    def product(left, right):
        depth = left.shape[1] // 2
        straight = dot(left[:, :depth], right, ((1,), (0,)))
        crossed = pltpu.roll(dot(left[:, depth:], right, ((1,), (0,))), wide, 1)
        low = lax.broadcasted_iota(jnp.int32, crossed.shape, 1) < wide
        return straight + jnp.where(low, crossed, -crossed)

    def block_product(left, block, right):
        every = left[:, :, block * 2 * rows : (block + 1) * 2 * rows].reshape(levels * out_rows, 2 * rows)
        return product(every, right).reshape(levels, out_rows, 2 * wide)

    def partial(chunk, group):
        left = turned[group]
        return product(left[:, : 2 * rows], w[chunk, 0]) + product(left[:, 2 * rows :], w[chunk, 1])

    def rows_of(target):
        return pl.multiple_of((2 * target + side) * out_rows, out_rows)

    def put(chunk, total):
        for part in range(2):
            for index in range(wide // 128):
                first = part * wide + index * 128
                out_ref[:, 2 * (chunk * wide // 128 + index) + part] = total[:, first : first + 128]

    def term(chunk, lane, slot, target, level_to, arrival=None):
        return remote(
            hp.at[chunk, pl.ds(rows_of(target), out_rows)], hr.at[chunk, lane, slot],
            h_send.at[0], h_recv.at[chunk, slot if arrival is None else arrival], {"tile": 2 * level_to + side},
        )

    def settle():
        for number in range(len(ROUTES)):
            guarded(sends[number], lambda number=number: route(number, 0, PIECES).wait_send())
        to_pair(OWN, PAIR, 0).wait_send()
        to_pair(ACROSS, PAIR_ACROSS, 1).wait_send()
        image_copy.wait_send()

        @pl.loop(0, FAR)
        def _(slot):
            @pl.when(exists(slot))
            def _():
                couple_copy(slot).wait_send()

        @pl.when(has_far)
        def _():
            for part in range(parts):
                far_copy(part).wait_send()

        if ends:
            @pl.when(gives)
            def _():
                for index in range(chunks - given):
                    gift_copy(index, 0).wait_send()

            @pl.when(takes)
            def _():
                for index in range(chunks - given):
                    gift_copy(index, 1).wait_send()
                to_pair(end_slot, PAIR_END, 2).wait_send()
                to_pair(end_across, PAIR_END_ACROSS, 3).wait_send()

        remote(w.at[:, 0], w.at[:, 1], w_send.at[0], w_recv.at[0], across).wait_send()

        def sent(count):
            rows_sent = hp.at[:count, pl.ds(0, (levels - 1) * out_rows)]
            remote(rows_sent, rows_sent, h_send.at[0], h_recv.at[0, 0], across).wait_send()

        if levels > 1:
            if given == chunks:
                sent(chunks)
            else:
                pl.when(gives)(lambda: sent(given))
                pl.when(takes)(lambda: sent(chunks))

    if short_line(out_rows, levels):
        depths = level, levels - 1 - level

        def total(chunk):
            tot[chunk] = block_product(turned, 0, w[chunk, 0])
            w_copy(chunk).wait_recv()
            tot[chunk] += block_product(turned, 1, w[chunk, 1])

        def place(target):
            return pl.ds(rows_of(target), out_rows)

        def far(lane, number):
            return levels - 1 - number if lane == 0 else number

        def passing(chunk, lane, target, number):
            arrival = number if number < levels - 2 else 2 + lane
            return term(chunk, lane, target, target, level + 1 - 2 * lane, arrival)

        def begin(chunk, numbers):
            for lane in range(2):
                for number in numbers:
                    target = far(lane, number)

                    @pl.when(depths[lane] == 0)
                    def _(lane=lane, target=target, number=number):
                        hp[chunk, place(target)] = tot[chunk, target].astype(BF16)
                        passing(chunk, lane, target, number).start()

        def beside(chunk):
            for lane in range(2):
                target = far(lane, 0)

                @pl.when(depths[lane] == 2)
                def _(lane=lane, target=target):
                    hp[chunk, place(target)] = tot[chunk, target].astype(BF16)
                    term(chunk, lane, levels, target, target, 0).start()

        def add_on(chunk, number):
            for lane in range(2):
                target = far(lane, number)

                @pl.when(depths[lane] == 1)
                def _(lane=lane, target=target):
                    value = tot[chunk, target]
                    if chunk < given:
                        passing(chunk, lane, target, number).wait_recv()
                        value = value + hr[chunk, lane, target].astype(F32)
                    hp[chunk, place(target)] = value.astype(BF16)
                    term(chunk, lane, target, target, target, 2 + lane).start()

        def pass_gift(index):
            @pl.when(takes)
            def _():
                gift_copy(index, 0).wait_recv()
                gift_copy(index, 1).start()

        def use_gift(index, block):
            @pl.when(takes)
            def _():
                if block:
                    gift_copy(index, 1).wait_recv()
                more = block_product(turned_end, block, gift[index, block])
                for target in range(1, levels - 1):
                    tot[given + index, target] += more[target]
                far_end = jnp.where(level == 1, levels - 1, 0)
                tot[given + index, far_end] += jnp.where(level == 1, more[levels - 1], more[0])

        distant = range(levels - 2)

        for chunk in range(chunks + 1):
            if chunk < chunks:
                total(chunk)
                if chunk < given:
                    begin(chunk, distant)
                if levels > 3:
                    beside(chunk)
            if ends and chunk == GIVE_AT:
                give(has_far)
            if chunk == given - 1 and levels > 1:
                for done in range(given):
                    begin(done, (levels - 2,))
            if ends and chunk == TURN_AT:
                turn_end()
            if 0 <= chunk - PASS_AT < chunks - given:
                pass_gift(chunk - PASS_AT)
            if ends and chunk == given:
                use_gift(0, 0)
                add_on(chunk - 1, 0)
                use_gift(0, 1)
                for number, done in ((0, chunk), (1, chunk - 1), (1, chunk)):
                    add_on(done, number)
            elif 0 < chunk < given or given == chunks == chunk:
                for number in distant:
                    add_on(chunk - 1, number)

        for chunk in range(chunks):
            if chunk == chunks - 1:
                settle()
            for lane, slot, arrival, there in (
                (0, level, 2, depths[0] > (1 if chunk >= given else 0)),
                (1, level, 3, depths[1] > (1 if chunk >= given else 0)),
                (0, levels, 0, depths[0] > 2), (1, levels, 0, depths[1] > 2),
            ):
                @pl.when(there)
                def _(chunk=chunk, lane=lane, slot=slot, arrival=arrival):
                    term(chunk, lane, slot, level, level, arrival).wait_recv()
                    tot[chunk, level] += hr[chunk, lane, slot].astype(F32)
            if wide % 128 == 0:
                put(chunk, tot[chunk, level])
            elif chunk % 2:
                for part, value in enumerate(halves(tot[chunk - 1, level], tot[chunk, level])):
                    out_ref[:, chunk - 1 + part] = value
    else:
        for chunk in range(chunks):
            w_copy(chunk).wait_recv()
            if span != out_rows:
                @pl.loop(0, hp.shape[1] // span)
                def _(group):
                    column = pl.multiple_of(group * span, span)
                    hp[chunk, pl.ds(column, span)] = partial(chunk, group).astype(BF16)

            @pl.loop(0, levels - 1)
            def _(number):
                target = other_level(number)
                if span == out_rows:
                    hp[chunk, pl.ds(rows_of(target), out_rows)] = partial(chunk, target).astype(BF16)
                term(chunk, 0, level, target, target).start()

            if span == out_rows:
                hp[chunk, pl.ds(rows_of(level), out_rows)] = partial(chunk, level).astype(BF16)

        for chunk in range(chunks):
            def add(number, total):
                sender = other_level(number)
                term(chunk, 0, sender, level, sender).wait_recv()
                return total + hr[chunk, 0, sender].astype(F32)

            put(chunk, lax.fori_loop(0, levels - 1, add, hp[chunk, pl.ds(rows_of(level), out_rows)].astype(F32)))

        settle()

def shards(count_tile, green, direction, partners, counts):
    tile_dev, kmax = partners.shape
    rows, half = green.shape[1:]
    sources = direction.shape[2]
    out_rows = sources // count_tile
    levels = count_tile // 2
    chunks = SHORT_CHUNKS if short_line(out_rows, levels) else CHUNKS
    wide = half // chunks
    parts = 2 if rows % 256 == 0 else 1
    lanes = 2 if short_line(out_rows, levels) else 1
    anywhere = pl.BlockSpec(memory_space=pl.ANY)
    local = pl.BlockSpec(memory_space=pltpu.VMEM)
    dma = pltpu.SemaphoreType.DMA
    out = pl.pallas_call(
        functools.partial(kernel, count_tile),
        out_shape=jax.ShapeDtypeStruct((out_rows, half // 64, 128), F32),
        in_specs=[anywhere] * 4,
        out_specs=local,
        scratch_shapes=[
            pltpu.SMEM((tile_dev, kmax), jnp.int32),
            pltpu.SMEM((tile_dev,), jnp.int32),
            pltpu.VMEM((PAIR_END_ACROSS + 1, 2, rows, half), BF16),
            pltpu.VMEM((2, 2, half, half), BF16),
            pltpu.VMEM((2 * rows, half), BF16),
            pltpu.VMEM((2, rows, half), F32),
            pltpu.VMEM((2, rows, half), F32),
            pltpu.VMEM((FAR, 2, rows, rows), F32),
            pltpu.VMEM((FAR, 2, rows, rows), F32),
            pltpu.VMEM((2 * rows, half), F32),
            pltpu.VMEM((chunks, 2, rows, 2 * wide), BF16),
            pltpu.VMEM((levels if out_rows >= 128 else sources // 128, max(out_rows, 128), 4 * rows), BF16),
            pltpu.VMEM((chunks, sources, 2 * wide), BF16),
            pltpu.VMEM((chunks, lanes, levels + 1, out_rows, 2 * wide), BF16),
            dma((5,)),
            dma((2,)),
            dma((len(ROUTES),)),
            dma((len(RELAYED), PIECES)),
            dma((len(FINAL) + 1,)),
            dma((FAR + 2,)),
            dma((FAR + 2,)),
            dma((4,)),
            dma((4,)),
            dma((1,)),
            dma((chunks,)),
            dma((1,)),
            dma((chunks, 4 if lanes == 2 else levels + 1)),
            pltpu.VMEM((chunks, levels, out_rows, 2 * wide) if lanes == 2 else (1, 1, 8, 128), F32),
            pltpu.VMEM((GIFTS, 2, rows, 2 * wide), BF16),
            pltpu.VMEM((levels, out_rows, 4 * rows) if lanes == 2 else (1, 16, 128), BF16),
            dma((GIFTS, 2)),
            dma((GIFTS, 2)),
            pltpu.VMEM((2, parts, 2, rows, rows // parts), F32),
        ],
        compiler_params=pltpu.CompilerParams(
            collective_id=0, has_side_effects=True, vmem_limit_bytes=56 * 1024 * 1024
        ),
    )(green, direction, partners, counts)
    out = out.reshape(out_rows, half // 128, 2, 128)
    return jnp.swapaxes(out, 1, 2).reshape(out_rows, 2, half)


def solution(mesh):
    in_specs = (
        P(None, ("freq", "tile"), "src"),
        P(None, ("freq", "src"), None),
        P(("freq", "tile"), None),
        P(("freq", "tile")),
    )
    out_specs = P(("freq", "tile"), None, "src")
    body = functools.partial(shards, mesh.shape["tile"])
    return jax.shard_map(body, mesh=mesh, in_specs=in_specs, out_specs=out_specs, check_vma=False)
```
